32 devices in a mesh: face: 4 (over z), tile: 8 (over y, x, core).
Axes of the slice: x: 2, y: 2, z: 4, core: 2. Of those that a mesh axis runs over, the one named last changes fastest.
Arguments:
- fields: bfloat16 [12, 128, 128, 256], P('face', 'tile'), may hold values from -6 to 6
- cotangent: bfloat16 [12, 128, 128, 256], P('face', 'tile'), may hold values from -6 to 6
- dw_kernel: float32 [256, 49], P('tile'), may hold values from -0.875 to 0.875
- dw_bias: float32 [256], P('tile'), may hold values from -3 to 3
- norm_gain: float32 [256], replicated, may hold values from 0.1 to 1.9
- norm_bias: float32 [256], replicated, may hold values from -3 to 3
- proj_in: bfloat16 [256, 1024], replicated, may hold values from -0.375 to 0.375
- bias_in: float32 [1024], replicated, may hold values from -3 to 3
- proj_out: bfloat16 [1024, 256], replicated, may hold values from -0.1875 to 0.1875
- bias_out: float32 [256], replicated, may hold values from -3 to 3
- layer_scale: float32 [256], replicated, may hold values from 0.3 to 1.5
- strip_source: int32 [48], replicated, may hold values from 0 to 47, each once
- strip_flip: int32 [48], replicated, may hold values 0 or 1
Outputs:
- section_out: bfloat16 [12, 128, 128, 256], P('face', 'tile')
- field_grad: bfloat16 [12, 128, 128, 256], P('face', 'tile')
The draws below stay inside these ranges and needn't reach their ends.
Inputs may be any that keep to these rules, and one draw needn't show every extreme that they name: `strip_source`: entry 4 f + e names strip 4 f' + e', the edge e' of base face f' of the same sample whose rim pads edge e of face f; every strip is named exactly once.
All inputs are finite; a program needn't handle non-finite values.
Results may differ from the reference program's by a relative error of at most 0.0057.
Values may be sent and summed in bfloat16 or wider, within the bound.
No kernel may reach another device: no remote copies, remote signals or barrier semaphores. Data moves between devices by JAX's collectives and lax.ppermute only.
A program may use at most 192 MiB of HBM per device.

```python
import math
import jax
import jax.numpy as jnp
from jax import lax

S = 128
C = 256
HID = 1024
FS = 12


def with_ends(values, key, least, top_value):
    index_at = [jax.random.randint(jax.random.fold_in(key, axis), (), 0, length) for axis, length in enumerate(values.shape)]
    main_axis = values.shape.index(max(values.shape))
    beside = index_at[:main_axis] + [(index_at[main_axis] + 1) % values.shape[main_axis]] + index_at[main_axis + 1:]
    return values.at[tuple(index_at)].set(least).at[tuple(beside)].set(top_value)


def steps_of(key, dims, pieces, smallest, high):
    def one(position, blocks):
        draws = jax.random.uniform(jax.random.fold_in(jax.random.fold_in(key, 6), position), (blocks,), jnp.float32, smallest / len(pieces), high / len(pieces))
        return jnp.repeat(jnp.exp(draws), dims[position] // blocks).reshape((-1,) + (1,) * (len(dims) - position - 1))

    factor_of = one(*pieces[0])
    for cut in pieces[1:]:
        factor_of = factor_of * one(*cut)
    return factor_of


def normal_values(key, dims, width, limit, cuts=(), kind=jnp.bfloat16):
    entries = width * jax.random.normal(key, dims, jnp.float32)
    if cuts:
        entries = entries * steps_of(key, dims, cuts, -0.22, 0.18)
    return jnp.clip(entries, -limit, limit).astype(kind)


def setup_inputs(seed: int = 0) -> dict:
    key_of = jax.random.split(jax.random.key(seed), 14)
    fields = normal_values(key_of[0], (FS, S, S, C), 1.0, 6.0, ((0, 4), (1, 8)))
    cotangent = normal_values(key_of[1], (FS, S, S, C), 1.0, 6.0, ((0, 4), (1, 8)))
    dw_kernel = normal_values(key_of[2], (C, 49), 49 ** -0.5, 0.875, ((0, 8),), jnp.float32)
    dw_bias = normal_values(key_of[3], (C,), 0.5, 3.0, ((0, 8),), jnp.float32)
    norm_gain = jnp.clip(1.0 + 0.18 * jax.random.normal(key_of[4], (C,), jnp.float32), 0.1, 1.9)
    norm_bias = normal_values(key_of[5], (C,), 0.5, 3.0, (), jnp.float32)
    proj_in = normal_values(key_of[6], (C, HID), C ** -0.5, 0.375)
    bias_in = normal_values(key_of[7], (HID,), 0.5, 3.0, (), jnp.float32)
    proj_out = normal_values(key_of[8], (HID, C), HID ** -0.5, 0.1875)
    bias_out = normal_values(key_of[9], (C,), 0.5, 3.0, (), jnp.float32)
    layer_scale = jnp.clip(jnp.exp(jax.random.uniform(key_of[10], (C,), jnp.float32, math.log(0.3), math.log(1.5))), 0.3, 1.5)
    strip_source = jax.random.permutation(key_of[11], 48).astype(jnp.int32)
    strip_flip = with_ends((jax.random.randint(key_of[12], (48,), 0, 2) < 1).astype(jnp.int32), jax.random.fold_in(key_of[12], 1), 0, 1)
    return dict(fields=fields, cotangent=cotangent, dw_kernel=dw_kernel, dw_bias=dw_bias, norm_gain=norm_gain, norm_bias=norm_bias, proj_in=proj_in, bias_in=bias_in, proj_out=proj_out, bias_out=bias_out, layer_scale=layer_scale, strip_source=strip_source, strip_flip=strip_flip)


EPSILON = 1e-06
GELU_SCALE = 0.7978845608028654
GELU_CUBIC = 0.044715

def gelu_value(pre):
    inner = GELU_SCALE * (pre + GELU_CUBIC * pre * pre * pre)
    return 0.5 * pre * (1.0 + jnp.tanh(inner))

def gelu_slope(pre):
    tanh_val = jnp.tanh(GELU_SCALE * (pre + GELU_CUBIC * pre * pre * pre))
    return 0.5 * (1.0 + tanh_val) + 0.5 * pre * (1.0 - tanh_val * tanh_val) * GELU_SCALE * (1.0 + 3.0 * GELU_CUBIC * pre * pre)

def edge_rims(face):
    top = face[0:3]
    bottom = face[::-1][0:3]
    left = jnp.transpose(face[:, 0:3], (1, 0, 2))
    right = jnp.transpose(face[:, ::-1][:, 0:3], (1, 0, 2))
    return jnp.stack([top, bottom, left, right])

def pad_face(face, strips):
    chans = face.shape[2]
    left = jnp.transpose(strips[2][::-1], (1, 0, 2))
    right = jnp.transpose(strips[3], (1, 0, 2))
    middle = jnp.concatenate([left, face, right], axis=1)
    corner = jnp.zeros((3, 3, chans), face.dtype)
    top = jnp.concatenate([corner, strips[0][::-1], corner], axis=1)
    bottom = jnp.concatenate([corner, strips[1], corner], axis=1)
    return jnp.concatenate([top, middle, bottom], axis=0)

def depthwise(padded, kernel, bias):
    size = padded.shape[0] - 6
    total = jnp.zeros((size, size, padded.shape[2]), jnp.float32) + bias
    for row_tap in range(7):
        for col_tap in range(7):
            window = padded[row_tap:row_tap + size, col_tap:col_tap + size].astype(jnp.float32)
            total = total + window * kernel[:, row_tap * 7 + col_tap]
    return total

def reference(fields, cotangent, dw_kernel, dw_bias, norm_gain, norm_bias, proj_in, bias_in, proj_out, bias_out, layer_scale, strip_source, strip_flip):
    count = fields.shape[0]
    size = fields.shape[1]
    chans = fields.shape[3]
    rims = jax.vmap(edge_rims)(fields)
    sample = jnp.arange(count, dtype=jnp.int32)
    reader = (sample % 12)[:, None] * 4 + jnp.arange(4, dtype=jnp.int32)[None, :]
    source = ((sample // 12)[:, None] * 48 + strip_source[reader]).astype(jnp.int32)
    mirror = (strip_flip[reader] == 1)[:, :, None, None, None]
    picked = rims.reshape(count * 4, 3, size, chans)[source.reshape(-1)].reshape(count, 4, 3, size, chans)
    strips = jnp.where(mirror, picked[:, :, :, ::-1], picked)

    def one_sample(packed):
        face, strip_set, cot_face = packed

        def convolve(face_wide, strips_wide):
            return depthwise(pad_face(face_wide, strips_wide), dw_kernel, dw_bias)
        conv_wide, pullback = jax.vjp(convolve, face.astype(jnp.float32), strip_set.astype(jnp.float32))
        conv = conv_wide.astype(jnp.bfloat16)
        cells = conv.reshape(-1, chans).astype(jnp.float32)
        mean = lax.optimization_barrier(jnp.mean(cells, axis=-1, keepdims=True))
        centred = cells - mean
        inv = lax.rsqrt(lax.optimization_barrier(jnp.mean(centred * centred, axis=-1, keepdims=True)) + EPSILON)
        nhat = centred * inv
        normed = (nhat * norm_gain + norm_bias).astype(jnp.bfloat16)
        pre = jnp.dot(normed, proj_in, preferred_element_type=jnp.float32) + bias_in
        act = gelu_value(pre).astype(jnp.bfloat16)
        mlp = jnp.dot(act, proj_out, preferred_element_type=jnp.float32) + bias_out
        result = (face.reshape(-1, chans).astype(jnp.float32) + layer_scale * mlp).astype(jnp.bfloat16)
        dmix = (layer_scale * cot_face.reshape(-1, chans).astype(jnp.float32)).astype(jnp.bfloat16)
        dact = jnp.dot(dmix, proj_out.T, preferred_element_type=jnp.float32)
        dpre = (dact * gelu_slope(pre)).astype(jnp.bfloat16)
        dnorm = jnp.dot(dpre, proj_in.T, preferred_element_type=jnp.float32) * norm_gain
        dconv = inv * (dnorm - lax.optimization_barrier(jnp.mean(dnorm, axis=-1, keepdims=True)) - nhat * lax.optimization_barrier(jnp.mean(dnorm * nhat, axis=-1, keepdims=True)))
        dconv = dconv.astype(jnp.bfloat16)
        face_grad, strip_grad = pullback(dconv.reshape(size, size, chans).astype(jnp.float32))
        return (result.reshape(size, size, chans), face_grad, strip_grad)
    section_out, face_grads, strip_grads = lax.map(one_sample, (fields, strips, cotangent))
    strip_grads = jnp.where(mirror, strip_grads[:, :, :, ::-1], strip_grads)
    owned = jnp.zeros((count * 4, 3, size, chans), jnp.float32)
    owned = owned.at[source.reshape(-1)].add(strip_grads.reshape(count * 4, 3, size, chans))
    owned = owned.reshape(count, 4, 3, size, chans)
    total = face_grads
    total = total.at[:, 0:3].add(owned[:, 0])
    total = total.at[:, size - 3:].add(owned[:, 1][:, ::-1])
    total = total.at[:, :, 0:3].add(jnp.transpose(owned[:, 2], (0, 2, 1, 3)))
    total = total.at[:, :, size - 3:].add(jnp.transpose(owned[:, 3][:, ::-1], (0, 2, 1, 3)))
    conv_grad = total.astype(jnp.bfloat16)
    field_grad = (cotangent.astype(jnp.float32) + conv_grad.astype(jnp.float32)).astype(jnp.bfloat16)
    return (section_out, field_grad)
```

```python
import functools

import jax
import jax.numpy as jnp
from jax import lax
from jax.experimental import pallas as pl
from jax.experimental.pallas import tpu as pltpu
from jax.sharding import PartitionSpec as P

EPSILON = 1e-06
GELU_SCALE = 0.7978845608028654
GELU_CUBIC = 0.044715


def gelu_value(pre):
    inner = GELU_SCALE * (pre + GELU_CUBIC * pre * pre * pre)
    return 0.5 * pre * (1.0 + jnp.tanh(inner))


def gelu_slope(pre):
    tanh_val = jnp.tanh(GELU_SCALE * (pre + GELU_CUBIC * pre * pre * pre))
    return 0.5 * (1.0 + tanh_val) + 0.5 * pre * (1.0 - tanh_val * tanh_val) * GELU_SCALE * (
        1.0 + 3.0 * GELU_CUBIC * pre * pre
    )


def to_channels(cells):
    turned = jnp.transpose(cells, (0, 3, 1, 2))
    return lax.all_to_all(turned, "tile", split_axis=1, concat_axis=2, tiled=True)


def to_cells(planes):
    moved = lax.all_to_all(planes, "tile", split_axis=2, concat_axis=1, tiled=True)
    return jnp.transpose(moved, (0, 2, 3, 1))


def rims_of(planes):
    top = planes[:, :, 0:3, :]
    bottom = planes[:, :, ::-1, :][:, :, 0:3, :]
    left = jnp.swapaxes(planes[:, :, :, 0:3], 2, 3)
    right = jnp.swapaxes(planes[:, :, :, ::-1][:, :, :, 0:3], 2, 3)
    return jnp.stack([top, bottom, left, right], axis=1)


def edge_kernels(taps):
    kernel = taps.reshape(taps.shape[0], 7, 7)
    swapped = jnp.swapaxes(kernel, 1, 2)
    return jnp.stack([kernel, kernel[:, ::-1, :], swapped, swapped[:, ::-1, :]])


def edge_grads(band, kernels):
    size = band.shape[-1]
    padded = jnp.pad(band.astype(jnp.float32), ((0, 0), (0, 0), (0, 0), (0, 0), (3, 3)))
    layers = []
    for depth in range(3):
        total = jnp.zeros(band.shape[:3] + (size,), jnp.float32)
        for inner in range(3 - depth):
            for along in range(7):
                weight = kernels[:, :, 2 - depth - inner, along][None, :, :, None]
                total = total + weight * padded[:, :, :, inner, 6 - along : 6 - along + size]
        layers.append(total)
    return jnp.stack(layers, axis=3)


def grouped_conv(planes_wide, taps):
    chans = taps.shape[0]
    return lax.conv_general_dilated(
        planes_wide,
        taps.reshape(chans, 1, 7, 7),
        (1, 1),
        "VALID",
        dimension_numbers=("NCHW", "OIHW", "NCHW"),
        feature_group_count=chans,
        precision=lax.Precision.HIGHEST,
    )


def reader_tables(sample, strip_source, strip_flip):
    reader = (sample % 12)[:, None] * 4 + jnp.arange(4, dtype=jnp.int32)[None, :]
    source = (sample // 12)[:, None] * 48 + strip_source[reader]
    return (source, strip_flip[reader] == 1)


def shards(
    fields,
    cotangent,
    dw_kernel,
    dw_bias,
    norm_gain,
    norm_bias,
    proj_in,
    bias_in,
    proj_out,
    bias_out,
    layer_scale,
    strip_source,
    strip_flip,
):
    slots = fields.shape[0]
    size = fields.shape[2]
    chans = fields.shape[3]
    total_samples = slots * lax.axis_size("face")
    first = lax.axis_index("face") * slots
    own_samples = first + jnp.arange(slots, dtype=jnp.int32)
    source, mirror = reader_tables(own_samples, strip_source, strip_flip)
    planes = to_channels(fields)
    local_ch = planes.shape[1]
    all_rims = lax.all_gather(rims_of(planes), "face", axis=0, tiled=True)
    picked = jnp.take(
        all_rims.reshape(total_samples * 4, local_ch, 3, size), source.reshape(-1), axis=0
    )
    picked = picked.reshape(slots, 4, local_ch, 3, size)
    strips = jnp.where(mirror[:, :, None, None, None], picked[..., ::-1], picked)
    left = jnp.swapaxes(strips[:, 2][:, :, ::-1, :], 2, 3)
    right = jnp.swapaxes(strips[:, 3], 2, 3)
    middle = jnp.concatenate([left, planes, right], axis=3)
    edge_pad = ((0, 0), (0, 0), (0, 0), (3, 3))
    top = jnp.pad(strips[:, 0][:, :, ::-1, :], edge_pad)
    bottom = jnp.pad(strips[:, 1], edge_pad)
    padded = jnp.concatenate([top, middle, bottom], axis=2)
    conv_sum = grouped_conv(padded.astype(jnp.float32), dw_kernel) + dw_bias[None, :, None, None]
    conv = to_cells(conv_sum.astype(jnp.bfloat16))
    cells = conv.reshape(-1, chans).astype(jnp.float32)
    mean = jnp.mean(cells, axis=-1, keepdims=True)
    centred = cells - mean
    inv = lax.rsqrt(jnp.mean(centred * centred, axis=-1, keepdims=True) + EPSILON)
    nhat = centred * inv
    normed = (nhat * norm_gain + norm_bias).astype(jnp.bfloat16)
    pre = jnp.dot(normed, proj_in, preferred_element_type=jnp.float32) + bias_in
    act = gelu_value(pre).astype(jnp.bfloat16)
    mlp = jnp.dot(act, proj_out, preferred_element_type=jnp.float32) + bias_out
    section_out = (fields.reshape(-1, chans).astype(jnp.float32) + layer_scale * mlp).astype(
        jnp.bfloat16
    )
    dmix = (layer_scale * cotangent.reshape(-1, chans).astype(jnp.float32)).astype(jnp.bfloat16)
    dact = lax.dot_general(
        dmix, proj_out, (((1,), (1,)), ((), ())), preferred_element_type=jnp.float32
    )
    dpre = (dact * gelu_slope(pre)).astype(jnp.bfloat16)
    dnorm = (
        lax.dot_general(dpre, proj_in, (((1,), (1,)), ((), ())), preferred_element_type=jnp.float32)
        * norm_gain
    )
    dconv = inv * (
        dnorm
        - jnp.mean(dnorm, axis=-1, keepdims=True)
        - nhat * jnp.mean(dnorm * nhat, axis=-1, keepdims=True)
    )
    dconv = dconv.astype(jnp.bfloat16).reshape(fields.shape)
    dplanes = to_channels(dconv)
    dpadded = jnp.pad(dplanes.astype(jnp.float32), ((0, 0), (0, 0), (3, 3), (3, 3)))
    flipped = dw_kernel.reshape(local_ch, 7, 7)[:, ::-1, ::-1].reshape(local_ch, 49)
    interior = grouped_conv(dpadded, flipped)
    kernels = edge_kernels(dw_kernel)
    band = rims_of(dplanes)
    flat_width = local_ch * 3 * size
    strip_grad = edge_grads(band, kernels)
    strip_grad = jnp.where(mirror[:, :, None, None, None], strip_grad[..., ::-1], strip_grad)
    targets = jnp.arange(total_samples * 4, dtype=jnp.int32)
    onehot = (targets[:, None] == source.reshape(-1)[None, :]).astype(jnp.float32)
    spread = jnp.dot(
        onehot, strip_grad.reshape(slots * 4, flat_width), precision=lax.Precision.HIGHEST
    )
    spread = spread.reshape(total_samples, 4, local_ch, 3, size)
    owned = lax.psum_scatter(
        spread.astype(jnp.bfloat16), "face", scatter_dimension=0, tiled=True
    ).astype(jnp.float32)
    interior = interior.at[:, :, 0:3, :].add(owned[:, 0])
    interior = interior.at[:, :, size - 3 :, :].add(owned[:, 1][:, :, ::-1, :])
    interior = interior.at[:, :, :, 0:3].add(jnp.swapaxes(owned[:, 2], 2, 3))
    interior = interior.at[:, :, :, size - 3 :].add(jnp.swapaxes(owned[:, 3][:, :, ::-1, :], 2, 3))
    conv_grad = to_cells(interior.astype(jnp.bfloat16))
    field_grad = (cotangent.astype(jnp.float32) + conv_grad.astype(jnp.float32)).astype(
        jnp.bfloat16
    )
    return (section_out.reshape(fields.shape), field_grad)

DEPTH = 3
TAPS = 7
SUB = 8
LANES = 128


def conv_rows(xs, w, half, col, rows_out, row_base):
    acc = [None] * rows_out
    for q in range(TAPS):
        taps = [w[half, pl.ds(TAPS * p + q, 1), :] for p in range(TAPS)]
        for row in range(rows_out + TAPS - 1):
            x = xs[half, row_base + row, pl.ds(col + q, SUB), :]
            for p in range(TAPS):
                i = row - p
                if 0 <= i < rows_out:
                    part = x * taps[p]
                    acc[i] = part if acc[i] is None else acc[i] + part
    return acc


def fill(xs, x_ref, top_ref, bot_ref, lead):
    rows, width = x_ref.shape[1], x_ref.shape[2]
    for half in range(x_ref.shape[3] // LANES):
        lanes = pl.ds(half * LANES, LANES)
        xs[half, pl.ds(0, DEPTH), pl.ds(lead, width), :] = top_ref[0, :, :, lanes].astype(jnp.float32)
        xs[half, pl.ds(DEPTH + rows, DEPTH), pl.ds(lead, width), :] = bot_ref[0, :, :, lanes].astype(
            jnp.float32
        )

        def one(row, carry):
            xs[half, DEPTH + row, pl.ds(lead, width), :] = x_ref[0, row, :, lanes].astype(jnp.float32)
            return carry

        lax.fori_loop(0, rows, one, 0)


def conv_forward_kernel(x_ref, top_ref, bot_ref, left_ref, right_ref, w_ref, out_ref, xs):
    rows, width, chans = x_ref.shape[1:]
    fill(xs, x_ref, top_ref, bot_ref, SUB)
    for half in range(chans // LANES):
        lanes = pl.ds(half * LANES, LANES)
        xs[half, :, pl.ds(0, SUB), :] = left_ref[0, :, :, lanes].astype(jnp.float32)
        xs[half, :, pl.ds(SUB + width, SUB), :] = right_ref[0, :, :, lanes].astype(jnp.float32)
    step = min(rows, 16)
    for half in range(chans // LANES):
        lanes = pl.ds(half * LANES, LANES)

        def one(block, carry):
            start = pl.multiple_of(block * SUB, SUB)
            for base in range(0, rows, step):
                acc = conv_rows(xs, w_ref, half, start + SUB - DEPTH, step, base)
                for i in range(step):
                    out_ref[0, base + i, pl.ds(start, SUB), lanes] = (
                        acc[i] + w_ref[half, pl.ds(TAPS * TAPS, 1), :]
                    )
            return carry

        lax.fori_loop(0, width // SUB, one, 0)


def conv_backward_kernel(x_ref, top_ref, bot_ref, w_ref, out_ref, left_ref, right_ref, above_ref, below_ref, xs):
    rows, width, chans = x_ref.shape[1:]
    lead = 2 * SUB
    for half in range(chans // LANES):
        xs[half, :, pl.ds(0, lead), :] = jnp.zeros((rows + 2 * DEPTH, lead, LANES), jnp.float32)
        xs[half, :, pl.ds(lead + width, lead), :] = jnp.zeros((rows + 2 * DEPTH, lead, LANES), jnp.float32)
    fill(xs, x_ref, top_ref, bot_ref, lead)
    step = min(rows, 16)
    for half in range(chans // LANES):
        lanes = pl.ds(half * LANES, LANES)

        def one(block, carry):
            start = pl.multiple_of(block * SUB, SUB)
            for base in range(0, rows, step):
                acc = conv_rows(xs, w_ref, half, start + lead - DEPTH, step, base)
                for i in range(step):
                    out_ref[0, base + i, pl.ds(start, SUB), lanes] = acc[i]
            above = [None] * DEPTH
            below = [None] * DEPTH
            for q in range(TAPS):
                for edge in range(DEPTH):
                    x_top = xs[half, DEPTH + edge, pl.ds(start + lead - DEPTH + q, SUB), :]
                    x_bot = xs[half, DEPTH + rows - 1 - edge, pl.ds(start + lead - DEPTH + q, SUB), :]
                    for d in range(DEPTH - edge):
                        p = edge + d + DEPTH + 1
                        up = x_top * w_ref[half, pl.ds(TAPS * p + q, 1), :]
                        down = x_bot * w_ref[half, pl.ds(TAPS * (TAPS - 1 - p) + q, 1), :]
                        above[d] = up if above[d] is None else above[d] + up
                        below[d] = down if below[d] is None else below[d] + down
            for d in range(DEPTH):
                above_ref[0, d, pl.ds(start, SUB), lanes] = above[d]
                below_ref[0, d, pl.ds(start, SUB), lanes] = below[d]
            return carry

        lax.fori_loop(0, width // SUB, one, 0)
        for base in range(0, rows, step):
            for ref, start in ((left_ref, lead - SUB), (right_ref, lead + width)):
                acc = conv_rows(xs, w_ref, half, start - DEPTH, step, base)
                for i in range(step):
                    ref[0, base + i, :, lanes] = acc[i]


def cell_kernel(conv_ref, x_ref, cot_ref, vec_ref, bias_in_ref, w_in_ref, w_out_ref, w_out_t_ref, w_in_t_ref, out_ref, dconv_ref, *, chunk):
    chans = conv_ref.shape[1]
    gain, shift = vec_ref[0:1, :], vec_ref[1:2, :]
    bias_out, scale = vec_ref[2:3, :], vec_ref[3:4, :]
    hidden = w_in_ref.shape[1]
    piece = 256

    def one(block, carry):
        at = pl.ds(pl.multiple_of(block * chunk, chunk), chunk)
        cells = conv_ref[at, :].astype(jnp.bfloat16).astype(jnp.float32)
        mean = jnp.sum(cells, axis=-1, keepdims=True) * (1.0 / chans)
        centred = cells - mean
        inv = lax.rsqrt(jnp.sum(centred * centred, axis=-1, keepdims=True) * (1.0 / chans) + EPSILON)
        nhat = centred * inv
        normed = (nhat * gain + shift).astype(jnp.bfloat16)
        dmix = (scale * cot_ref[at, :].astype(jnp.float32)).astype(jnp.bfloat16)
        mlp = None
        dnorm = None
        for first in range(0, hidden, piece):
            cut = pl.ds(first, piece)
            pre = jnp.dot(normed, w_in_ref[:, cut], preferred_element_type=jnp.float32)
            pre = pre + bias_in_ref[0:1, cut]
            dact = jnp.dot(dmix, w_out_t_ref[:, cut], preferred_element_type=jnp.float32)
            square = pre * pre
            tanh_val = jnp.tanh(pre * (GELU_SCALE + (GELU_SCALE * GELU_CUBIC) * square))
            lifted = 0.5 + 0.5 * tanh_val
            act = (pre * lifted).astype(jnp.bfloat16)
            bend = (0.5 * GELU_SCALE) * pre + (1.5 * GELU_SCALE * GELU_CUBIC) * (pre * square)
            slope = lifted + (1.0 - tanh_val * tanh_val) * bend
            dpre = (dact * slope).astype(jnp.bfloat16)
            mlp_part = jnp.dot(act, w_out_ref[cut, :], preferred_element_type=jnp.float32)
            dnorm_part = jnp.dot(dpre, w_in_t_ref[cut, :], preferred_element_type=jnp.float32)
            mlp = mlp_part if mlp is None else mlp + mlp_part
            dnorm = dnorm_part if dnorm is None else dnorm + dnorm_part
        out_ref[at, :] = (x_ref[at, :].astype(jnp.float32) + scale * (mlp + bias_out)).astype(jnp.bfloat16)
        dnorm = dnorm * gain
        first_mean = jnp.sum(dnorm, axis=-1, keepdims=True) * (1.0 / chans)
        second_mean = jnp.sum(dnorm * nhat, axis=-1, keepdims=True) * (1.0 / chans)
        dconv_ref[at, :] = (inv * (dnorm - first_mean - nhat * second_mean)).astype(jnp.bfloat16)
        return carry

    lax.fori_loop(0, conv_ref.shape[0] // chunk, one, 0)


def join_kernel(grad_ref, cot_ref, top_ref, bot_ref, left_ref, right_ref, out_ref, total):
    rows, width, chans = grad_ref.shape[1:]
    total[...] = grad_ref[0]
    total[pl.ds(0, DEPTH)] += top_ref[0].astype(jnp.float32)
    total[pl.ds(rows - DEPTH, DEPTH)] += bot_ref[0].astype(jnp.float32)
    total[:, pl.ds(0, SUB), :] += left_ref[0].astype(jnp.float32)
    total[:, pl.ds(width - SUB, SUB), :] += right_ref[0].astype(jnp.float32)

    def one(row, carry):
        conv_grad = total[row].astype(jnp.bfloat16).astype(jnp.float32)
        out_ref[0, row] = (cot_ref[0, row].astype(jnp.float32) + conv_grad).astype(jnp.bfloat16)
        return carry

    lax.fori_loop(0, rows, one, 0)


def by_slot(shape):
    return pl.BlockSpec((1,) + tuple(shape[1:]), lambda s: (s,) + (0,) * (len(shape) - 1))


def whole(shape):
    return pl.BlockSpec(tuple(shape), lambda s: (0,) * len(shape))


def params():
    return pltpu.CompilerParams(vmem_limit_bytes=56 * 1024 * 1024)


def conv_forward(fields, top, bot, left, right, weights):
    slots, rows, width, chans = fields.shape
    ins = (fields, top, bot, left, right)
    return pl.pallas_call(
        conv_forward_kernel,
        grid=(slots,),
        in_specs=[by_slot(x.shape) for x in ins] + [whole(weights.shape)],
        out_specs=by_slot(fields.shape),
        out_shape=jax.ShapeDtypeStruct(fields.shape, jnp.float32),
        scratch_shapes=[
            pltpu.VMEM((chans // LANES, rows + 2 * DEPTH, width + 2 * SUB, LANES), jnp.float32)
        ],
        compiler_params=params(),
        name="conv_forward",
    )(*ins, weights)


def conv_backward(dconv, top, bot, weights):
    slots, rows, width, chans = dconv.shape
    ins = (dconv, top, bot)
    outs = [
        (slots, rows, width, chans),
        (slots, rows, SUB, chans),
        (slots, rows, SUB, chans),
        (slots, DEPTH, width, chans),
        (slots, DEPTH, width, chans),
    ]
    return pl.pallas_call(
        conv_backward_kernel,
        grid=(slots,),
        in_specs=[by_slot(x.shape) for x in ins] + [whole(weights.shape)],
        out_specs=[by_slot(s) for s in outs],
        out_shape=[jax.ShapeDtypeStruct(s, jnp.float32) for s in outs],
        scratch_shapes=[
            pltpu.VMEM((chans // LANES, rows + 2 * DEPTH, width + 4 * SUB, LANES), jnp.float32)
        ],
        compiler_params=params(),
        name="conv_backward",
    )(*ins, weights)


def cell_block(conv, fields, cotangent, vectors, bias_in, proj_in, proj_out):
    cells, chans = conv.shape
    block, chunk = 1024, 256
    tiled = pl.BlockSpec((block, chans), lambda s: (s, 0))
    rest = (vectors, bias_in, proj_in, proj_out, proj_out.T, proj_in.T)
    out = jax.ShapeDtypeStruct(conv.shape, jnp.bfloat16)
    return pl.pallas_call(
        functools.partial(cell_kernel, chunk=chunk),
        grid=(cells // block,),
        in_specs=[tiled] * 3 + [whole(x.shape) for x in rest],
        out_specs=[tiled, tiled],
        out_shape=[out, out],
        compiler_params=params(),
        name="cell_block",
    )(conv, fields, cotangent, *rest)


def join(grad, cotangent, top, bot, left, right):
    ins = (grad, cotangent, top, bot, left, right)
    return pl.pallas_call(
        join_kernel,
        grid=(grad.shape[0],),
        in_specs=[by_slot(x.shape) for x in ins],
        out_specs=by_slot(grad.shape),
        out_shape=jax.ShapeDtypeStruct(grad.shape, jnp.bfloat16),
        scratch_shapes=[pltpu.VMEM(grad.shape[1:], jnp.float32)],
        compiler_params=params(),
        name="join",
    )(*ins)


def face_all(blocks):
    groups = lax.axis_size("face")
    parts = [blocks]
    for step in range(1, groups):
        parts.append(lax.ppermute(blocks, "face", [(g, (g + step) % groups) for g in range(groups)]))
    return jnp.concatenate(parts, axis=0)


def exchange(ends, sides, index, flip):
    slots, _, width, chans = ends.shape
    tiles, groups = lax.axis_size("tile"), lax.axis_size("face")
    tile, group = lax.axis_index("tile"), lax.axis_index("face")
    rows = width // tiles
    send = jnp.moveaxis(ends.reshape(slots, DEPTH, tiles, rows, chans), 2, 0)
    got = lax.all_to_all(send, "tile", split_axis=0, concat_axis=0, tiled=True)
    rims = jnp.concatenate([jnp.stack([got[0], got[tiles - 1]], axis=1), sides], axis=1)
    strips = face_all(rims.reshape(slots * 4, DEPTH, rows, chans))
    per_group = slots * 4
    place = ((group - index // per_group) % groups) * per_group + index % per_group
    picked = jnp.take(strips, place.reshape(-1), axis=0).reshape(slots, 4, DEPTH, rows, chans)
    half = tiles // 2
    back = jnp.stack([picked[:, 0]] * half + [picked[:, 1]] * (tiles - half))
    back = lax.all_to_all(back, "tile", split_axis=0, concat_axis=0, tiled=True)
    end_flip = jnp.where(tile == 0, flip[:, 0], flip[:, 1])[:, None, None, None]
    new_ends = jnp.moveaxis(back, 0, 2).reshape(slots, DEPTH, width, chans)
    new_ends = jnp.where(end_flip, new_ends[:, :, ::-1], new_ends)
    mirrored = lax.ppermute(picked[:, 2:], "tile", [(t, tiles - 1 - t) for t in range(tiles)])
    new_sides = jnp.where(flip[:, 2:, None, None, None], mirrored[:, :, :, ::-1], picked[:, 2:])
    return new_ends, new_sides


def halo(first, last):
    tiles = lax.axis_size("tile")
    above = lax.ppermute(last, "tile", [(t, t + 1) for t in range(tiles - 1)])
    below = lax.ppermute(first, "tile", [(t + 1, t) for t in range(tiles - 1)])
    return above, below


def row_shards(
    fields,
    cotangent,
    dw_kernel,
    dw_bias,
    norm_gain,
    norm_bias,
    proj_in,
    bias_in,
    proj_out,
    bias_out,
    layer_scale,
    strip_source,
    strip_flip,
):
    slots, rows, width, chans = fields.shape
    tiles = lax.axis_size("tile")
    tile = lax.axis_index("tile")
    first_tile, last_tile = tile == 0, tile == tiles - 1
    own_samples = lax.axis_index("face") * slots + jnp.arange(slots, dtype=jnp.int32)
    source, mirror = reader_tables(own_samples, strip_source, strip_flip)
    entries = jnp.arange(48, dtype=jnp.int32)
    hits = strip_source[None, :] == entries[:, None]
    reader_of = jnp.sum(jnp.where(hits, entries[None, :], 0), axis=1)
    flip_of = jnp.sum(jnp.where(hits, strip_flip[None, :], 0), axis=1)
    own_strips = (own_samples % 12)[:, None] * 4 + jnp.arange(4, dtype=jnp.int32)[None, :]
    target = (own_samples // 12)[:, None] * 48 + reader_of[own_strips]
    target_mirror = flip_of[own_strips] == 1

    taps = jnp.concatenate([dw_kernel, dw_bias[:, None]], axis=1).T
    taps = lax.all_to_all(
        jnp.broadcast_to(taps[None], (tiles,) + taps.shape), "tile", split_axis=0, concat_axis=0, tiled=True
    )
    taps = jnp.moveaxis(taps, 0, 1).reshape(TAPS * TAPS + 1, chans)
    taps = jnp.pad(taps, ((0, 6), (0, 0)))
    weights = jnp.moveaxis(taps.reshape(-1, chans // LANES, LANES), 1, 0)
    turned = jnp.pad(weights[:, TAPS * TAPS - 1 :: -1], ((0, 0), (0, 7), (0, 0)))

    ends = jnp.where(first_tile, fields[:, :DEPTH], fields[:, : rows - DEPTH - 1 : -1])
    side_pair = jnp.stack([fields[:, :, :DEPTH], fields[:, :, : width - DEPTH - 1 : -1]], axis=1)
    sides = jnp.swapaxes(side_pair, 2, 3)
    above, below = halo(fields[:, :DEPTH], fields[:, rows - DEPTH :])
    new_ends, new_sides = exchange(ends, sides, source, mirror)
    side_above, side_below = halo(new_sides[:, :, :, :DEPTH], new_sides[:, :, :, rows - DEPTH :])
    tall = jnp.swapaxes(jnp.concatenate([side_above, new_sides, side_below], axis=3), 2, 3)
    left = jnp.pad(tall[:, 0, :, ::-1], ((0, 0), (0, 0), (SUB - DEPTH, 0), (0, 0)))
    right = jnp.pad(tall[:, 1], ((0, 0), (0, 0), (0, SUB - DEPTH), (0, 0)))
    top = jnp.where(first_tile, new_ends[:, ::-1], above)
    bot = jnp.where(last_tile, new_ends, below)
    conv = conv_forward(fields, top, bot, left, right, weights)
    vectors = jnp.stack([norm_gain, norm_bias, bias_out, layer_scale])
    flat = (-1, chans)
    section_out, dconv = cell_block(
        conv.reshape(flat), fields.reshape(flat), cotangent.reshape(flat), vectors, bias_in[None], proj_in, proj_out
    )
    dconv = dconv.reshape(fields.shape)
    above, below = halo(dconv[:, :DEPTH], dconv[:, rows - DEPTH :])
    grad, left, right, top, bot = conv_backward(dconv, above, below, turned)
    ends = jnp.where(first_tile, top, bot).astype(jnp.bfloat16)
    sides = jnp.stack([left[:, :, : SUB - DEPTH - 1 : -1], right[:, :, :DEPTH]], axis=1).astype(jnp.bfloat16)
    ends, sides = exchange(ends, jnp.swapaxes(sides, 2, 3), target, target_mirror)
    top = jnp.where(first_tile, ends, 0)
    bot = jnp.where(last_tile, ends[:, ::-1], 0)
    sides = jnp.swapaxes(sides, 2, 3)
    left = jnp.pad(sides[:, 0], ((0, 0), (0, 0), (0, SUB - DEPTH), (0, 0)))
    right = jnp.pad(sides[:, 1, :, ::-1], ((0, 0), (0, 0), (SUB - DEPTH, 0), (0, 0)))
    field_grad = join(grad, cotangent, top, bot, left, right)
    return (section_out.reshape(fields.shape), field_grad)


def block_of(fields, *rest):
    rows, chans = fields.shape[1], fields.shape[3]
    if rows % SUB == 0 and chans % LANES == 0 and fields.shape[2] % (2 * LANES // 2) == 0:
        return row_shards(fields, *rest)
    return shards(fields, *rest)


def solution(mesh):
    placed = (
        P("face", "tile", None, None),
        P("face", "tile", None, None),
        P("tile", None),
        P("tile"),
        P(),
        P(),
        P(),
        P(),
        P(),
        P(),
        P(),
        P(),
        P(),
    )
    return jax.shard_map(
        block_of,
        mesh=mesh,
        in_specs=placed,
        out_specs=(P("face", "tile", None, None), P("face", "tile", None, None)),
        check_vma=False,
    )
```

```python
import jax
import jax.numpy as jnp
from jax import lax
from jax.experimental import pallas as pl
from jax.experimental.pallas import tpu as pltpu
from jax.sharding import PartitionSpec as P

EPSILON = 1e-06
GELU_SCALE = 0.7978845608028654
GELU_CUBIC = 0.044715


def gelu_value(pre):
    inner = GELU_SCALE * (pre + GELU_CUBIC * pre * pre * pre)
    return 0.5 * pre * (1.0 + jnp.tanh(inner))


def gelu_slope(pre):
    tanh_val = jnp.tanh(GELU_SCALE * (pre + GELU_CUBIC * pre * pre * pre))
    return 0.5 * (1.0 + tanh_val) + 0.5 * pre * (1.0 - tanh_val * tanh_val) * GELU_SCALE * (
        1.0 + 3.0 * GELU_CUBIC * pre * pre
    )


def to_channels(cells):
    turned = jnp.transpose(cells, (0, 3, 1, 2))
    return lax.all_to_all(turned, "tile", split_axis=1, concat_axis=2, tiled=True)


def to_cells(planes):
    moved = lax.all_to_all(planes, "tile", split_axis=2, concat_axis=1, tiled=True)
    return jnp.transpose(moved, (0, 2, 3, 1))


def rims_of(planes):
    top = planes[:, :, 0:3, :]
    bottom = planes[:, :, ::-1, :][:, :, 0:3, :]
    left = jnp.swapaxes(planes[:, :, :, 0:3], 2, 3)
    right = jnp.swapaxes(planes[:, :, :, ::-1][:, :, :, 0:3], 2, 3)
    return jnp.stack([top, bottom, left, right], axis=1)


def edge_kernels(taps):
    kernel = taps.reshape(taps.shape[0], 7, 7)
    swapped = jnp.swapaxes(kernel, 1, 2)
    return jnp.stack([kernel, kernel[:, ::-1, :], swapped, swapped[:, ::-1, :]])


def edge_grads(band, kernels):
    size = band.shape[-1]
    padded = jnp.pad(band.astype(jnp.float32), ((0, 0), (0, 0), (0, 0), (0, 0), (3, 3)))
    layers = []
    for depth in range(3):
        total = jnp.zeros(band.shape[:3] + (size,), jnp.float32)
        for inner in range(3 - depth):
            for along in range(7):
                weight = kernels[:, :, 2 - depth - inner, along][None, :, :, None]
                total = total + weight * padded[:, :, :, inner, 6 - along : 6 - along + size]
        layers.append(total)
    return jnp.stack(layers, axis=3)


def grouped_conv(planes_wide, taps):
    chans = taps.shape[0]
    return lax.conv_general_dilated(
        planes_wide,
        taps.reshape(chans, 1, 7, 7),
        (1, 1),
        "VALID",
        dimension_numbers=("NCHW", "OIHW", "NCHW"),
        feature_group_count=chans,
        precision=lax.Precision.HIGHEST,
    )


def reader_tables(sample, strip_source, strip_flip):
    reader = (sample % 12)[:, None] * 4 + jnp.arange(4, dtype=jnp.int32)[None, :]
    source = (sample // 12)[:, None] * 48 + strip_source[reader]
    return (source, strip_flip[reader] == 1)


def shards(
    fields,
    cotangent,
    dw_kernel,
    dw_bias,
    norm_gain,
    norm_bias,
    proj_in,
    bias_in,
    proj_out,
    bias_out,
    layer_scale,
    strip_source,
    strip_flip,
):
    slots = fields.shape[0]
    size = fields.shape[2]
    chans = fields.shape[3]
    total_samples = slots * lax.axis_size("face")
    first = lax.axis_index("face") * slots
    own_samples = first + jnp.arange(slots, dtype=jnp.int32)
    source, mirror = reader_tables(own_samples, strip_source, strip_flip)
    planes = to_channels(fields)
    local_ch = planes.shape[1]
    all_rims = lax.all_gather(rims_of(planes), "face", axis=0, tiled=True)
    picked = jnp.take(
        all_rims.reshape(total_samples * 4, local_ch, 3, size), source.reshape(-1), axis=0
    )
    picked = picked.reshape(slots, 4, local_ch, 3, size)
    strips = jnp.where(mirror[:, :, None, None, None], picked[..., ::-1], picked)
    left = jnp.swapaxes(strips[:, 2][:, :, ::-1, :], 2, 3)
    right = jnp.swapaxes(strips[:, 3], 2, 3)
    middle = jnp.concatenate([left, planes, right], axis=3)
    edge_pad = ((0, 0), (0, 0), (0, 0), (3, 3))
    top = jnp.pad(strips[:, 0][:, :, ::-1, :], edge_pad)
    bottom = jnp.pad(strips[:, 1], edge_pad)
    padded = jnp.concatenate([top, middle, bottom], axis=2)
    conv_sum = grouped_conv(padded.astype(jnp.float32), dw_kernel) + dw_bias[None, :, None, None]
    conv = to_cells(conv_sum.astype(jnp.bfloat16))
    cells = conv.reshape(-1, chans).astype(jnp.float32)
    mean = jnp.mean(cells, axis=-1, keepdims=True)
    centred = cells - mean
    inv = lax.rsqrt(jnp.mean(centred * centred, axis=-1, keepdims=True) + EPSILON)
    nhat = centred * inv
    normed = (nhat * norm_gain + norm_bias).astype(jnp.bfloat16)
    pre = jnp.dot(normed, proj_in, preferred_element_type=jnp.float32) + bias_in
    act = gelu_value(pre).astype(jnp.bfloat16)
    mlp = jnp.dot(act, proj_out, preferred_element_type=jnp.float32) + bias_out
    section_out = (fields.reshape(-1, chans).astype(jnp.float32) + layer_scale * mlp).astype(
        jnp.bfloat16
    )
    dmix = (layer_scale * cotangent.reshape(-1, chans).astype(jnp.float32)).astype(jnp.bfloat16)
    dact = lax.dot_general(
        dmix, proj_out, (((1,), (1,)), ((), ())), preferred_element_type=jnp.float32
    )
    dpre = (dact * gelu_slope(pre)).astype(jnp.bfloat16)
    dnorm = (
        lax.dot_general(dpre, proj_in, (((1,), (1,)), ((), ())), preferred_element_type=jnp.float32)
        * norm_gain
    )
    dconv = inv * (
        dnorm
        - jnp.mean(dnorm, axis=-1, keepdims=True)
        - nhat * jnp.mean(dnorm * nhat, axis=-1, keepdims=True)
    )
    dconv = dconv.astype(jnp.bfloat16).reshape(fields.shape)
    dplanes = to_channels(dconv)
    dpadded = jnp.pad(dplanes.astype(jnp.float32), ((0, 0), (0, 0), (3, 3), (3, 3)))
    flipped = dw_kernel.reshape(local_ch, 7, 7)[:, ::-1, ::-1].reshape(local_ch, 49)
    interior = grouped_conv(dpadded, flipped)
    kernels = edge_kernels(dw_kernel)
    band = rims_of(dplanes)
    flat_width = local_ch * 3 * size
    strip_grad = edge_grads(band, kernels)
    strip_grad = jnp.where(mirror[:, :, None, None, None], strip_grad[..., ::-1], strip_grad)
    targets = jnp.arange(total_samples * 4, dtype=jnp.int32)
    onehot = (targets[:, None] == source.reshape(-1)[None, :]).astype(jnp.float32)
    spread = jnp.dot(
        onehot, strip_grad.reshape(slots * 4, flat_width), precision=lax.Precision.HIGHEST
    )
    spread = spread.reshape(total_samples, 4, local_ch, 3, size)
    owned = lax.psum_scatter(
        spread.astype(jnp.bfloat16), "face", scatter_dimension=0, tiled=True
    ).astype(jnp.float32)
    interior = interior.at[:, :, 0:3, :].add(owned[:, 0])
    interior = interior.at[:, :, size - 3 :, :].add(owned[:, 1][:, :, ::-1, :])
    interior = interior.at[:, :, :, 0:3].add(jnp.swapaxes(owned[:, 2], 2, 3))
    interior = interior.at[:, :, :, size - 3 :].add(jnp.swapaxes(owned[:, 3][:, :, ::-1, :], 2, 3))
    conv_grad = to_cells(interior.astype(jnp.bfloat16))
    field_grad = (cotangent.astype(jnp.float32) + conv_grad.astype(jnp.float32)).astype(
        jnp.bfloat16
    )
    return (section_out.reshape(fields.shape), field_grad)

DEPTH = 3
TAPS = 7
SUB = 8
LANES = 128
SIDE = 16


def load_taps(w, half, q):
    return [w[half, pl.ds(TAPS * p + q, 1), :] for p in range(TAPS)]


def plus(total, part):
    return part if total is None else total + part


def widen_rows(xs, at, ref, rows, lead):
    width = ref.shape[2]
    for half in range(ref.shape[3] // LANES):
        lanes = pl.ds(half * LANES, LANES)

        def one(row, carry):
            xs[half, at + row, pl.ds(lead, width), :] = ref[0, row, :, lanes].astype(jnp.float32)
            return carry

        if rows > DEPTH:
            lax.fori_loop(0, rows, one, 0)
        else:
            for row in range(rows):
                one(row, 0)


def clear_pads(xs, width):
    halves, rows = xs.shape[:2]
    for half in range(halves):
        xs[half, :, pl.ds(0, SUB), :] = jnp.zeros((rows, SUB, LANES), jnp.float32)
        xs[half, :, pl.ds(SUB + width, SUB), :] = jnp.zeros((rows, SUB, LANES), jnp.float32)


def conv_partial_kernel(x_ref, w_ref, out_ref, xs):
    rows, width, chans = x_ref.shape[1:]
    clear_pads(xs, width)
    widen_rows(xs, 0, x_ref, rows, SUB)
    wide = 2
    for half in range(chans // LANES):
        lanes = pl.ds(half * LANES, LANES)

        def one(block, carry):
            start = pl.multiple_of(block * (SUB * wide), SUB * wide)
            acc = [[None] * rows for _ in range(wide)]
            for q in range(TAPS):
                taps = load_taps(w_ref, half, q)
                for row in range(rows):
                    for b in range(wide):
                        x = xs[half, row, pl.ds(start + SUB * (b + 1) - DEPTH + q, SUB), :]
                        for p in range(TAPS):
                            i = row + DEPTH - p
                            if 0 <= i < rows:
                                acc[b][i] = plus(acc[b][i], x * taps[p])
            bias = w_ref[half, pl.ds(TAPS * TAPS, 1), :]
            for b in range(wide):
                for i in range(rows):
                    out_ref[0, i, pl.ds(start + SUB * b, SUB), lanes] = acc[b][i] + bias
            return carry

        lax.fori_loop(0, width // (SUB * wide), one, 0)


def row_parts(xh, w, half, col):
    head = [None] * DEPTH
    tail = [None] * DEPTH
    for q in range(TAPS):
        for h in range(DEPTH):
            up = xh[half, h, pl.ds(col + SUB - DEPTH + q, SUB), :]
            down = xh[half, DEPTH + h, pl.ds(col + SUB - DEPTH + q, SUB), :]
            for i in range(h + 1):
                head[i] = plus(head[i], up * w[half, pl.ds(TAPS * (h - i) + q, 1), :])
            for k in range(DEPTH - h):
                tail[k] = plus(tail[k], down * w[half, pl.ds(TAPS * (h + k + 4) + q, 1), :])
    return head, tail


def end_parts(xh, w, half, col, first):
    out = [None] * DEPTH
    for q in range(TAPS):
        for h in range(DEPTH):
            x = xh[half, jnp.where(first, h, 2 * DEPTH - 1 - h), pl.ds(col + SUB - DEPTH + q, SUB), :]
            for d in range(h + 1):
                p = jnp.where(first, h - d, TAPS - 1 - h + d)
                out[d] = plus(out[d], x * w[half, pl.ds(TAPS * p + q, 1), :])
    return out


def column_parts(xc, w, half, starts):
    rows = xc.shape[1] - 2 * DEPTH
    acc = [None] * rows
    for q, start in starts:
        taps = load_taps(w, half, q)
        for row in range(rows + 2 * DEPTH):
            x = xc[half, row, pl.ds(start, SUB), :]
            for p in range(TAPS):
                if 0 <= row - p < rows:
                    acc[row - p] = plus(acc[row - p], x * taps[p])
    return acc


def cells_of(cells, x, cot, vec, bias_in, w_in, w_out, w_out_t, w_in_t):
    chans = cells.shape[1]
    gain, shift, bias_out, scale = (vec[k : k + 1, :] for k in range(4))
    hidden = w_in.shape[1]
    piece = 256
    cells = cells.astype(jnp.bfloat16).astype(jnp.float32)
    mean = jnp.sum(cells, axis=-1, keepdims=True) * (1.0 / chans)
    centred = cells - mean
    inv = lax.rsqrt(jnp.sum(centred * centred, axis=-1, keepdims=True) * (1.0 / chans) + EPSILON)
    nhat = centred * inv
    normed = (nhat * gain + shift).astype(jnp.bfloat16)
    dmix = (scale * cot.astype(jnp.float32)).astype(jnp.bfloat16)
    mlp = None
    dnorm = None
    for first in range(0, hidden, piece):
        cut = pl.ds(first, piece)
        pre = jnp.dot(normed, w_in[:, cut], preferred_element_type=jnp.float32) + bias_in[0:1, cut]
        dact = jnp.dot(dmix, w_out_t[:, cut], preferred_element_type=jnp.float32)
        square = pre * pre
        tanh_val = jnp.tanh(pre * (GELU_SCALE + (GELU_SCALE * GELU_CUBIC) * square))
        lifted = 0.5 + 0.5 * tanh_val
        act = (pre * lifted).astype(jnp.bfloat16)
        bend = pre * ((0.5 * GELU_SCALE) + (1.5 * GELU_SCALE * GELU_CUBIC) * square)
        slope = lifted + (1.0 - tanh_val * tanh_val) * bend
        dpre = (dact * slope).astype(jnp.bfloat16)
        mlp = plus(mlp, jnp.dot(act, w_out[cut, :], preferred_element_type=jnp.float32))
        dnorm = plus(dnorm, jnp.dot(dpre, w_in_t[cut, :], preferred_element_type=jnp.float32))
    section = (x.astype(jnp.float32) + scale * (mlp + bias_out)).astype(jnp.bfloat16)
    dnorm = dnorm * gain
    first_mean = jnp.sum(dnorm, axis=-1, keepdims=True) * (1.0 / chans)
    second_mean = jnp.sum(dnorm * nhat, axis=-1, keepdims=True) * (1.0 / chans)
    dconv = (inv * (dnorm - first_mean - nhat * second_mean)).astype(jnp.bfloat16)
    return section, dconv


def edge_kernel(
    flags, cl, cr, ce, xl, xr, xe, gl, gr, ge, top, bot, left, right, w, wt, vec, bi, wi, wo, wot, wit,
    sl, sr, se, dl, dr, de, tb, xh, xcl, xcr, lrs, ends,
):
    rows, chans = cl.shape[1], cl.shape[3]
    width = top.shape[2]
    inner = width - 2 * SIDE
    mats = (vec, bi, wi, wo, wot, wit)
    first = flags[0] == 1
    clear_pads(xh, width)
    widen_rows(xh, 0, top, DEPTH, SUB)
    widen_rows(xh, DEPTH, bot, DEPTH, SUB)
    for half in range(chans // LANES):
        lanes = pl.ds(half * LANES, LANES)
        xcl[half, :, pl.ds(0, SUB), :] = left[0, :, :, lanes].astype(jnp.float32)
        xcl[half, :, pl.ds(SUB, SUB), :] = jnp.zeros((rows + 2 * DEPTH, SUB, LANES), jnp.float32)
        xcr[half, :, pl.ds(0, SUB), :] = jnp.zeros((rows + 2 * DEPTH, SUB, LANES), jnp.float32)
        xcr[half, :, pl.ds(SUB, SUB), :] = right[0, :, :, lanes].astype(jnp.float32)
    lrs[0] = cl[0]
    lrs[1] = cr[0]
    for half in range(chans // LANES):
        lanes = pl.ds(half * LANES, LANES)
        near = column_parts(xcl, w, half, [(q, SUB - DEPTH + q) for q in range(DEPTH)])
        far = column_parts(xcr, w, half, [(q, q - DEPTH) for q in range(4, TAPS)])
        for i in range(rows):
            lrs[0, i, pl.ds(0, SUB), lanes] += near[i]
            lrs[1, i, pl.ds(SIDE - SUB, SUB), lanes] += far[i]
        for side in range(2):
            for b in range(0, SIDE, SUB):
                head, tail = row_parts(xh, w, half, b + side * (width - SIDE))
                for d in range(DEPTH):
                    lrs[side, d, pl.ds(b, SUB), lanes] += head[d]
                    lrs[side, rows - 1 - d, pl.ds(b, SUB), lanes] += tail[d]
    flat = (2 * rows * SIDE, chans)
    both = lambda a, b: jnp.stack([a[0], b[0]]).reshape(flat)
    section, dconv = cells_of(lrs[...].reshape(flat), both(xl, xr), both(gl, gr), *mats)
    section = section.reshape(2, rows, SIDE, chans)
    dconv = dconv.reshape(2, rows, SIDE, chans)
    sl[0] = section[0]
    sr[0] = section[1]
    dl[0] = dconv[0]
    dr[0] = dconv[1]

    @pl.when(flags[0] + flags[1] > 0)
    def _():
        at = [jnp.where(first, d, SUB - 1 - d) for d in range(DEPTH)]
        whole_at = [jnp.where(first, d, rows - 1 - d) for d in range(DEPTH)]
        mid = pl.ds(SIDE, inner)
        for d in range(DEPTH):
            ends[d] = ce[0, at[d], mid, :]
        for half in range(chans // LANES):
            lanes = pl.ds(half * LANES, LANES)

            def one(block, carry):
                start = pl.multiple_of(block * SUB, SUB)
                parts = end_parts(xh, w, half, start + SIDE, first)
                for d in range(DEPTH):
                    ends[d, pl.ds(start, SUB), lanes] += parts[d]
                return carry

            lax.fori_loop(0, inner // SUB, one, 0)
        rim = lambda ref: jnp.stack([ref[0, at[d], mid, :] for d in range(DEPTH)]).reshape(DEPTH * inner, chans)
        section, dconv = cells_of(ends[...].reshape(DEPTH * inner, chans), rim(xe), rim(ge), *mats)
        se[0] = section.reshape(DEPTH, inner, chans)
        dconv = dconv.reshape(DEPTH, inner, chans)
        de[0] = dconv
        for half in range(chans // LANES):
            lanes = pl.ds(half * LANES, LANES)
            for d in range(DEPTH):
                xh[half, d, pl.ds(SUB, SIDE), :] = dl[0, whole_at[d], :, lanes].astype(jnp.float32)
                xh[half, d, pl.ds(SUB + SIDE, inner), :] = de[0, d, :, lanes].astype(jnp.float32)
                xh[half, d, pl.ds(SUB + SIDE + inner, SIDE), :] = dr[0, whole_at[d], :, lanes].astype(jnp.float32)

            def one_strip(block, carry):
                start = pl.multiple_of(block * SUB, SUB)
                out = [None] * DEPTH
                for q in range(TAPS):
                    for edge in range(DEPTH):
                        x = xh[half, edge, pl.ds(start + SUB - DEPTH + q, SUB), :]
                        for d in range(DEPTH - edge):
                            p = jnp.where(first, edge + d + 4, 2 - edge - d)
                            out[d] = plus(out[d], x * wt[half, pl.ds(TAPS * p + q, 1), :])
                for d in range(DEPTH):
                    xh[half, DEPTH + d, pl.ds(start + SUB, SUB), :] = out[d]
                return carry

            lax.fori_loop(0, width // SUB, one_strip, 0)
            for d in range(DEPTH):
                tb[0, d, :, lanes] = xh[half, DEPTH + d, pl.ds(SUB, width), :].astype(jnp.bfloat16)


def strip_kernel(left, right, wt, near_ref, far_ref, xcl, xcr):
    rows, chans = near_ref.shape[1], near_ref.shape[3]
    for half in range(chans // LANES):
        lanes = pl.ds(half * LANES, LANES)
        zeros = jnp.zeros((rows + 2 * DEPTH, SUB, LANES), jnp.float32)
        xcl[half, :, pl.ds(0, SUB), :] = zeros
        xcl[half, :, pl.ds(SUB, SUB), :] = left[0, :, :, lanes].astype(jnp.float32)
        xcr[half, :, pl.ds(0, SUB), :] = right[0, :, :, lanes].astype(jnp.float32)
        xcr[half, :, pl.ds(SUB, SUB), :] = zeros
    for half in range(chans // LANES):
        lanes = pl.ds(half * LANES, LANES)
        near = column_parts(xcl, wt, half, [(q, q - DEPTH) for q in range(4, TAPS)])
        far = column_parts(xcr, wt, half, [(q, SUB - DEPTH + q) for q in range(DEPTH)])
        for i in range(rows):
            near_ref[0, i, :, lanes] = near[i]
            far_ref[0, i, :, lanes] = far[i]


def interior_kernel(
    flags, conv, x, cot, top, bot, sl, sr, se, dl, dr, de, w, vec, bi, wi, wo, wot, wit, sec, dc, xh, cs
):
    rows, width, chans = conv.shape[1:]
    inner = width - 2 * SIDE
    mid = pl.ds(SIDE, inner)
    mats = (vec, bi, wi, wo, wot, wit)
    for full, near, far in ((sec, sl, sr), (dc, dl, dr)):
        full[0, :, pl.ds(0, SIDE), :] = near[0]
        full[0, :, pl.ds(width - SIDE, SIDE), :] = far[0]
    clear_pads(xh, width)
    widen_rows(xh, 0, top, DEPTH, SUB)
    widen_rows(xh, DEPTH, bot, DEPTH, SUB)
    last = rows - DEPTH
    cs[pl.ds(0, DEPTH)] = conv[0, pl.ds(0, DEPTH), mid, :]
    cs[pl.ds(DEPTH, DEPTH)] = conv[0, pl.ds(last, DEPTH), mid, :]
    for half in range(chans // LANES):
        lanes = pl.ds(half * LANES, LANES)

        def one(block, carry):
            start = pl.multiple_of(block * SUB, SUB)
            head, tail = row_parts(xh, w, half, start + SIDE)
            for d in range(DEPTH):
                cs[d, pl.ds(start, SUB), lanes] += head[d]
                cs[2 * DEPTH - 1 - d, pl.ds(start, SUB), lanes] += tail[d]
            return carry

        lax.fori_loop(0, inner // SUB, one, 0)

    at_end = flags[0] + flags[1] > 0

    @pl.when(jnp.logical_not(at_end))
    def _():
        flat = (2 * DEPTH * inner, chans)
        pick = lambda ref: jnp.concatenate([ref[0, pl.ds(0, DEPTH), mid, :], ref[0, pl.ds(last, DEPTH), mid, :]]).reshape(flat)
        section, dconv = cells_of(cs[...].reshape(flat), pick(x), pick(cot), *mats)
        for full, value in ((sec, section), (dc, dconv)):
            value = value.reshape(2 * DEPTH, inner, chans)
            full[0, pl.ds(0, DEPTH), mid, :] = value[:DEPTH]
            full[0, pl.ds(last, DEPTH), mid, :] = value[DEPTH:]

    @pl.when(at_end)
    def _():
        flat = (DEPTH * inner, chans)
        first = flags[0] == 1
        base = jnp.where(first, last, 0)
        rim = pl.ds(base, DEPTH)
        section, dconv = cells_of(
            cs[pl.ds(jnp.where(first, DEPTH, 0), DEPTH)].reshape(flat),
            x[0, rim, mid, :].reshape(flat),
            cot[0, rim, mid, :].reshape(flat),
            *mats,
        )
        for full, value, done in ((sec, section, se), (dc, dconv, de)):
            full[0, rim, mid, :] = value.reshape(DEPTH, inner, chans)
            for d in range(DEPTH):
                full[0, jnp.where(first, d, rows - 1 - d), mid, :] = done[0, d]

    free = rows - 2 * DEPTH
    step = free // 2

    def some(block, carry):
        flat = (step * inner, chans)
        these = pl.ds(DEPTH + block * step, step)
        section, dconv = cells_of(
            conv[0, these, mid, :].reshape(flat), x[0, these, mid, :].reshape(flat), cot[0, these, mid, :].reshape(flat), *mats
        )
        sec[0, these, mid, :] = section.reshape(step, inner, chans)
        dc[0, these, mid, :] = dconv.reshape(step, inner, chans)
        return carry

    lax.fori_loop(0, 2, some, 0)


def join_kernel(grad, cot, above, below, top, bot, left, right, wt, out, xh, total):
    rows, width, chans = grad.shape[1:]
    clear_pads(xh, width)
    widen_rows(xh, 0, above, DEPTH, SUB)
    widen_rows(xh, DEPTH, below, DEPTH, SUB)
    total[...] = grad[0]
    for half in range(chans // LANES):
        lanes = pl.ds(half * LANES, LANES)

        def one(block, carry):
            start = pl.multiple_of(block * SUB, SUB)
            head, tail = row_parts(xh, wt, half, start)
            for d in range(DEPTH):
                total[d, pl.ds(start, SUB), lanes] += head[d]
                total[rows - 1 - d, pl.ds(start, SUB), lanes] += tail[d]
            return carry

        lax.fori_loop(0, width // SUB, one, 0)
    total[pl.ds(0, DEPTH)] += top[0].astype(jnp.float32)
    total[pl.ds(rows - DEPTH, DEPTH)] += bot[0].astype(jnp.float32)
    total[:, pl.ds(0, SUB), :] += left[0].astype(jnp.float32)
    total[:, pl.ds(width - SUB, SUB), :] += right[0].astype(jnp.float32)

    def finish(row, carry):
        conv_grad = total[row].astype(jnp.bfloat16).astype(jnp.float32)
        out[0, row] = (cot[0, row].astype(jnp.float32) + conv_grad).astype(jnp.bfloat16)
        return carry

    lax.fori_loop(0, rows, finish, 0)


def by_slot(x, base=0):
    return pl.BlockSpec((1,) + tuple(x.shape[1:]), lambda s, *_: (s + base if base else s,) + (0,) * (len(x.shape) - 1))


def whole(x):
    return pl.BlockSpec(tuple(x.shape), lambda s, *_: (0,) * len(x.shape))


def run(kernel, name, span, ins, specs, outs, scratch, flags=None, micros=10, into=()):
    base, slots = span
    prefetch = () if flags is None else (flags,)
    first = len(prefetch) + len(ins)

    def body(*refs):
        return kernel(*refs[:first], *refs[first + len(into) :])

    return pl.pallas_call(
        body,
        grid_spec=pltpu.PrefetchScalarGridSpec(
            num_scalar_prefetch=len(prefetch),
            grid=(slots,),
            in_specs=specs + [pl.BlockSpec(memory_space=pl.ANY)] * len(into),
            out_specs=[by_slot(o, base) for o in outs],
            scratch_shapes=[pltpu.VMEM(s, jnp.float32) for s in scratch],
        ),
        out_shape=list(outs),
        input_output_aliases={first + k: k for k in range(len(into))},
        compiler_params=pltpu.CompilerParams(vmem_limit_bytes=60 * 1024 * 1024),
        cost_estimate=pl.CostEstimate(
            flops=micros * 1_000_000_000, transcendentals=0, bytes_accessed=sum(o.size * 2 for o in outs)
        ),
        name=name,
    )(*prefetch, *ins, *into)


def conv_partial(x, weights, name, span, into=()):
    slots, rows, width, chans = x.shape
    out = jax.ShapeDtypeStruct(x.shape, jnp.float32)
    pads = (chans // LANES, rows, width + 2 * SUB, LANES)
    specs = [by_slot(x, span[0]), whole(weights)]
    return run(conv_partial_kernel, name, span, (x, weights), specs, [out], [pads], micros=9 * span[1], into=into)[0]


def face_all(blocks):
    groups = lax.axis_size("face")
    parts = [blocks]
    for step in range(1, groups):
        parts.append(lax.ppermute(blocks, "face", [(g, (g + step) % groups) for g in range(groups)]))
    return jnp.stack(parts)


def spread_ends(ends, rider=None):
    slots, _, width, chans = ends.shape
    tiles = lax.axis_size("tile")
    rows = width // tiles
    send = jnp.moveaxis(ends.reshape(slots, DEPTH, tiles, rows, chans), 2, 0).reshape(tiles, -1, chans)
    if rider is not None:
        send = jnp.concatenate([send, jnp.broadcast_to(rider[None], (tiles,) + rider.shape)], axis=1)
    got = lax.all_to_all(send, "tile", split_axis=0, concat_axis=0, tiled=True)
    count = slots * DEPTH * rows
    found = jnp.stack([got[0, :count], got[tiles - 1, :count]]).reshape(2, slots, DEPTH, rows, chans)
    return jnp.moveaxis(found, 0, 1), got[:, count:]


def in_three(values):
    parts = []
    for _ in range(3):
        part = lax.reduce_precision(values, 8, 7)
        parts.append(part.astype(jnp.bfloat16))
        values = values - part
    return jnp.stack(parts)


def pick(all_ends, all_sides, index):
    groups, slots, _, _, rows, chans = all_ends.shape
    flat = (groups * slots * 2, DEPTH, rows, chans)
    strips = jnp.concatenate([all_ends.reshape(flat), all_sides.reshape(flat)])
    group, slot, edge = index // (slots * 4), index // 4 % slots, index % 4
    back = (lax.axis_index("face") - group) % groups
    place = jnp.where(edge < 2, back, groups + back) * (slots * 2) + slot * 2 + edge % 2
    return jnp.take(strips, place.reshape(-1), axis=0).reshape(slots, 4, DEPTH, rows, chans)


def settle(picked, flip, reach):
    slots, _, _, rows, chans = picked.shape
    tiles = lax.axis_size("tile")
    tile = lax.axis_index("tile")
    half = tiles // 2
    back = jnp.stack([picked[:, 0]] * half + [picked[:, 1]] * (tiles - half))
    back = lax.all_to_all(back, "tile", split_axis=0, concat_axis=0, tiled=True)
    end_flip = jnp.where(tile == 0, flip[:, 0], flip[:, 1])[:, None, None, None]
    new_ends = jnp.moveaxis(back, 0, 2).reshape(slots, DEPTH, tiles * rows, chans)
    new_ends = jnp.where(end_flip, new_ends[:, :, ::-1], new_ends)
    side_flip = flip[:, 2:, None, None, None]
    found = picked[:, 2:]
    mirrored = lax.ppermute(found, "tile", [(t, tiles - 1 - t) for t in range(tiles)])
    new_sides = jnp.where(side_flip, mirrored[:, :, :, ::-1], found)
    if reach:
        head, tail = found[:, :, :, :reach], found[:, :, :, rows - reach :]
        above, below = halo(head, tail)
        above_turned = lax.ppermute(head, "tile", [(t, tiles - t) for t in range(1, tiles)])
        below_turned = lax.ppermute(tail, "tile", [(t, tiles - 2 - t) for t in range(tiles - 1)])
        above = jnp.where(side_flip, above_turned[:, :, :, ::-1], above)
        below = jnp.where(side_flip, below_turned[:, :, :, ::-1], below)
        new_sides = jnp.concatenate([above, new_sides, below], axis=3)
    return new_ends, new_sides


def halo(first, last):
    tiles = lax.axis_size("tile")
    above = lax.ppermute(last, "tile", [(t, t + 1) for t in range(tiles - 1)])
    below = lax.ppermute(first, "tile", [(t + 1, t) for t in range(tiles - 1)])
    return above, below


def row_shards(
    fields,
    cotangent,
    dw_kernel,
    dw_bias,
    norm_gain,
    norm_bias,
    proj_in,
    bias_in,
    proj_out,
    bias_out,
    layer_scale,
    strip_source,
    strip_flip,
):
    slots, rows, width, chans = fields.shape
    tiles = lax.axis_size("tile")
    tile = lax.axis_index("tile")
    first_tile, last_tile = tile == 0, tile == tiles - 1
    flags = jnp.stack([first_tile, last_tile]).astype(jnp.int32)
    own_samples = lax.axis_index("face") * slots + jnp.arange(slots, dtype=jnp.int32)
    source, mirror = reader_tables(own_samples, strip_source, strip_flip)
    entries = jnp.arange(48, dtype=jnp.int32)
    hits = strip_source[None, :] == entries[:, None]
    reader_of = jnp.sum(jnp.where(hits, entries[None, :], 0), axis=1)
    flip_of = jnp.sum(jnp.where(hits, strip_flip[None, :], 0), axis=1)
    own_strips = (own_samples % 12)[:, None] * 4 + jnp.arange(4, dtype=jnp.int32)[None, :]
    target = (own_samples // 12)[:, None] * 48 + reader_of[own_strips]
    target_mirror = flip_of[own_strips] == 1

    own_taps = jnp.concatenate([dw_kernel, dw_bias[:, None]], axis=1).T
    own_chans = own_taps.shape[1]
    taps_count = TAPS * TAPS + 1
    rider_rows = -(-3 * taps_count * own_chans // chans)
    rider_rows += -rider_rows % 8
    rider = in_three(own_taps).reshape(-1)
    rider = jnp.pad(rider, (0, rider_rows * chans - rider.size)).reshape(rider_rows, chans)
    ends = jnp.where(first_tile, fields[:, :DEPTH], fields[:, : rows - DEPTH - 1 : -1])
    near_ends, riders = spread_ends(ends, rider)
    riders = riders.reshape(tiles, -1)[:, : 3 * taps_count * own_chans].astype(jnp.float32)
    riders = riders.reshape(tiles, 3, taps_count, own_chans)
    taps = (riders[:, 0] + riders[:, 1]) + riders[:, 2]
    taps = jnp.moveaxis(taps, 0, 1).reshape(taps_count, chans)
    taps = jnp.pad(taps, ((0, 6), (0, 0)))
    weights = jnp.moveaxis(taps.reshape(-1, chans // LANES, LANES), 1, 0)
    turned = jnp.pad(weights[:, TAPS * TAPS - 1 :: -1], ((0, 0), (0, 7), (0, 0)))
    vectors = jnp.stack([norm_gain, norm_bias, bias_out, layer_scale])
    mats = (vectors, bias_in[None], proj_in, proj_out, proj_out.T, proj_in.T)

    side_pair = jnp.stack([fields[:, :, :DEPTH], fields[:, :, : width - DEPTH - 1 : -1]], axis=1)
    all_sides = face_all(jnp.swapaxes(side_pair, 2, 3))
    above, below = halo(fields[:, :DEPTH], fields[:, rows - DEPTH :])
    all_ends = face_all(near_ends)
    early, near_ends, all_sides = lax.optimization_barrier((fields, near_ends, all_sides))
    partial = conv_partial(early, weights, "conv_partial", (0, 2))
    partial, all_ends, above, below = lax.optimization_barrier((partial, all_ends, above, below))
    picked = pick(all_ends, all_sides, source)
    late, picked = lax.optimization_barrier((fields, picked))
    new_ends, sides = settle(picked, mirror, DEPTH)
    partial = conv_partial(late, weights, "conv_partial_rest", (2, slots - 2), (partial,))
    sides = jnp.swapaxes(sides, 2, 3)
    left = jnp.pad(sides[:, 0, :, ::-1], ((0, 0), (0, 0), (SUB - DEPTH, 0), (0, 0)))
    right = jnp.pad(sides[:, 1], ((0, 0), (0, 0), (0, SUB - DEPTH), (0, 0)))
    top = jnp.where(first_tile, new_ends[:, ::-1], above)
    bot = jnp.where(last_tile, new_ends, below)

    near_spec = pl.BlockSpec((1, rows, SIDE, chans), lambda s, f: (s, 0, 0, 0))
    far_spec = pl.BlockSpec((1, rows, SIDE, chans), lambda s, f: (s, 0, width // SIDE - 1, 0))
    end_spec = pl.BlockSpec((1, SUB, width, chans), lambda s, f: (s, f[1] * (rows // SUB - 1), 0, 0))
    side_out = jax.ShapeDtypeStruct((slots, rows, SIDE, chans), jnp.bfloat16)
    end_out = jax.ShapeDtypeStruct((slots, DEPTH, width - 2 * SIDE, chans), jnp.bfloat16)
    strip_out = jax.ShapeDtypeStruct((slots, DEPTH, width, chans), jnp.bfloat16)
    halves = chans // LANES
    halo_pads = (halves, 2 * DEPTH, width + 2 * SUB, LANES)
    side_pads = (halves, rows + 2 * DEPTH, 2 * SUB, LANES)
    extras = (top, bot, left, right)
    sl, sr, se, dl, dr, de, tb = run(
        edge_kernel,
        "edge_cells",
        (0, slots),
        (partial,) * 3 + (fields,) * 3 + (cotangent,) * 3 + extras + (weights, turned) + mats,
        [near_spec, far_spec, end_spec] * 3 + [by_slot(x) for x in extras] + [whole(x) for x in (weights, turned) + mats],
        [side_out, side_out, end_out, side_out, side_out, end_out, strip_out],
        [halo_pads, side_pads, side_pads, (2, rows, SIDE, chans), (DEPTH, width - 2 * SIDE, chans)],
        flags,
        micros=23,
    )

    outer = jnp.stack([dl[:, :, :SUB], dr[:, :, SIDE - SUB :]], axis=1)
    outer_above, outer_below = halo(outer[:, :, :DEPTH], outer[:, :, rows - DEPTH :])
    outer = jnp.concatenate([outer_above, outer, outer_below], axis=2)
    strip = jax.ShapeDtypeStruct((slots, rows, SUB, chans), jnp.float32)
    ins = (outer[:, 0], outer[:, 1])
    near, far = run(
        strip_kernel,
        "side_strips",
        (0, slots),
        ins + (turned,),
        [by_slot(x) for x in ins] + [whole(turned)],
        [strip, strip],
        [side_pads, side_pads],
    )
    side_pair = jnp.stack([near[:, :, : SUB - DEPTH - 1 : -1], far[:, :, :DEPTH]], axis=1).astype(jnp.bfloat16)
    near_ends, _ = spread_ends(tb)
    all_sides = face_all(jnp.swapaxes(side_pair, 2, 3))
    all_ends = face_all(near_ends)

    full = jax.ShapeDtypeStruct(fields.shape, jnp.bfloat16)
    ins = (partial, fields, cotangent, top, bot, sl, sr, se, dl, dr, de)
    done = ()
    for span, sign in (((0, 1), near), ((1, slots - 1), (near_ends, all_sides))):
        gated = lax.optimization_barrier((fields, sign))[0]
        ins = (partial, gated, cotangent, top, bot, sl, sr, se, dl, dr, de)
        done = run(
            interior_kernel,
            "interior_cells",
            span,
            ins + (weights,) + mats,
            [by_slot(x, span[0]) for x in ins] + [whole(x) for x in (weights,) + mats],
            [full, full],
            [halo_pads, (2 * DEPTH, width - 2 * SIDE, chans)],
            flags,
            micros=9 * span[1],
            into=done,
        )
    section_out, dconv = done
    dconv, all_ends = lax.optimization_barrier((dconv, all_ends))
    picked = pick(all_ends, all_sides, target)
    ends, sides = settle(picked, target_mirror, 0)
    above, below = halo(dconv[:, :DEPTH], dconv[:, rows - DEPTH :])
    early, picked = lax.optimization_barrier((dconv, picked))
    grad = conv_partial(early, turned, "conv_gradient", (0, 2))
    late, above, below, ends = lax.optimization_barrier((dconv, above, below, ends))
    grad = conv_partial(late, turned, "conv_gradient_rest", (2, slots - 2), (grad,))

    top = jnp.where(first_tile, ends, 0)
    bot = jnp.where(last_tile, ends[:, ::-1], 0)
    sides = jnp.swapaxes(sides, 2, 3)
    left = jnp.pad(sides[:, 0], ((0, 0), (0, 0), (0, SUB - DEPTH), (0, 0)))
    right = jnp.pad(sides[:, 1, :, ::-1], ((0, 0), (0, 0), (SUB - DEPTH, 0), (0, 0)))
    ins = (grad, cotangent, above, below, top, bot, left, right)
    field_grad = run(
        join_kernel,
        "join",
        (0, slots),
        ins + (turned,),
        [by_slot(x) for x in ins] + [whole(turned)],
        [full],
        [halo_pads, (rows, width, chans)],
    )[0]
    return (section_out, field_grad)


def block_of(fields, *rest):
    rows, width, chans = fields.shape[1:]
    if rows % SUB == 0 and rows <= 16 and chans % LANES == 0 and width % SIDE == 0 and width > 4 * SIDE:
        return row_shards(fields, *rest)
    return shards(fields, *rest)


def solution(mesh):
    placed = (
        P("face", "tile", None, None),
        P("face", "tile", None, None),
        P("tile", None),
        P("tile"),
        P(),
        P(),
        P(),
        P(),
        P(),
        P(),
        P(),
        P(),
        P(),
    )
    return jax.shard_map(
        block_of,
        mesh=mesh,
        in_specs=placed,
        out_specs=(P("face", "tile", None, None), P("face", "tile", None, None)),
        check_vma=False,
    )
```

```python
import jax
import jax.numpy as jnp
from jax import lax
from jax.experimental import pallas as pl
from jax.experimental.pallas import tpu as pltpu
from jax.sharding import PartitionSpec as P

EPSILON = 1e-06
GELU_SCALE = 0.7978845608028654
GELU_CUBIC = 0.044715


def gelu_value(pre):
    inner = GELU_SCALE * (pre + GELU_CUBIC * pre * pre * pre)
    return 0.5 * pre * (1.0 + jnp.tanh(inner))


def gelu_slope(pre):
    tanh_val = jnp.tanh(GELU_SCALE * (pre + GELU_CUBIC * pre * pre * pre))
    return 0.5 * (1.0 + tanh_val) + 0.5 * pre * (1.0 - tanh_val * tanh_val) * GELU_SCALE * (
        1.0 + 3.0 * GELU_CUBIC * pre * pre
    )


def to_channels(cells):
    turned = jnp.transpose(cells, (0, 3, 1, 2))
    return lax.all_to_all(turned, "tile", split_axis=1, concat_axis=2, tiled=True)


def to_cells(planes):
    moved = lax.all_to_all(planes, "tile", split_axis=2, concat_axis=1, tiled=True)
    return jnp.transpose(moved, (0, 2, 3, 1))


def rims_of(planes):
    top = planes[:, :, 0:3, :]
    bottom = planes[:, :, ::-1, :][:, :, 0:3, :]
    left = jnp.swapaxes(planes[:, :, :, 0:3], 2, 3)
    right = jnp.swapaxes(planes[:, :, :, ::-1][:, :, :, 0:3], 2, 3)
    return jnp.stack([top, bottom, left, right], axis=1)


def edge_kernels(taps):
    kernel = taps.reshape(taps.shape[0], 7, 7)
    swapped = jnp.swapaxes(kernel, 1, 2)
    return jnp.stack([kernel, kernel[:, ::-1, :], swapped, swapped[:, ::-1, :]])


def edge_grads(band, kernels):
    size = band.shape[-1]
    padded = jnp.pad(band.astype(jnp.float32), ((0, 0), (0, 0), (0, 0), (0, 0), (3, 3)))
    layers = []
    for depth in range(3):
        total = jnp.zeros(band.shape[:3] + (size,), jnp.float32)
        for inner in range(3 - depth):
            for along in range(7):
                weight = kernels[:, :, 2 - depth - inner, along][None, :, :, None]
                total = total + weight * padded[:, :, :, inner, 6 - along : 6 - along + size]
        layers.append(total)
    return jnp.stack(layers, axis=3)


def grouped_conv(planes_wide, taps):
    chans = taps.shape[0]
    return lax.conv_general_dilated(
        planes_wide,
        taps.reshape(chans, 1, 7, 7),
        (1, 1),
        "VALID",
        dimension_numbers=("NCHW", "OIHW", "NCHW"),
        feature_group_count=chans,
        precision=lax.Precision.HIGHEST,
    )


def reader_tables(sample, strip_source, strip_flip):
    reader = (sample % 12)[:, None] * 4 + jnp.arange(4, dtype=jnp.int32)[None, :]
    source = (sample // 12)[:, None] * 48 + strip_source[reader]
    return (source, strip_flip[reader] == 1)


def shards(
    fields,
    cotangent,
    dw_kernel,
    dw_bias,
    norm_gain,
    norm_bias,
    proj_in,
    bias_in,
    proj_out,
    bias_out,
    layer_scale,
    strip_source,
    strip_flip,
):
    slots = fields.shape[0]
    size = fields.shape[2]
    chans = fields.shape[3]
    total_samples = slots * lax.axis_size("face")
    first = lax.axis_index("face") * slots
    own_samples = first + jnp.arange(slots, dtype=jnp.int32)
    source, mirror = reader_tables(own_samples, strip_source, strip_flip)
    planes = to_channels(fields)
    local_ch = planes.shape[1]
    all_rims = lax.all_gather(rims_of(planes), "face", axis=0, tiled=True)
    picked = jnp.take(
        all_rims.reshape(total_samples * 4, local_ch, 3, size), source.reshape(-1), axis=0
    )
    picked = picked.reshape(slots, 4, local_ch, 3, size)
    strips = jnp.where(mirror[:, :, None, None, None], picked[..., ::-1], picked)
    left = jnp.swapaxes(strips[:, 2][:, :, ::-1, :], 2, 3)
    right = jnp.swapaxes(strips[:, 3], 2, 3)
    middle = jnp.concatenate([left, planes, right], axis=3)
    edge_pad = ((0, 0), (0, 0), (0, 0), (3, 3))
    top = jnp.pad(strips[:, 0][:, :, ::-1, :], edge_pad)
    bottom = jnp.pad(strips[:, 1], edge_pad)
    padded = jnp.concatenate([top, middle, bottom], axis=2)
    conv_sum = grouped_conv(padded.astype(jnp.float32), dw_kernel) + dw_bias[None, :, None, None]
    conv = to_cells(conv_sum.astype(jnp.bfloat16))
    cells = conv.reshape(-1, chans).astype(jnp.float32)
    mean = jnp.mean(cells, axis=-1, keepdims=True)
    centred = cells - mean
    inv = lax.rsqrt(jnp.mean(centred * centred, axis=-1, keepdims=True) + EPSILON)
    nhat = centred * inv
    normed = (nhat * norm_gain + norm_bias).astype(jnp.bfloat16)
    pre = jnp.dot(normed, proj_in, preferred_element_type=jnp.float32) + bias_in
    act = gelu_value(pre).astype(jnp.bfloat16)
    mlp = jnp.dot(act, proj_out, preferred_element_type=jnp.float32) + bias_out
    section_out = (fields.reshape(-1, chans).astype(jnp.float32) + layer_scale * mlp).astype(
        jnp.bfloat16
    )
    dmix = (layer_scale * cotangent.reshape(-1, chans).astype(jnp.float32)).astype(jnp.bfloat16)
    dact = lax.dot_general(
        dmix, proj_out, (((1,), (1,)), ((), ())), preferred_element_type=jnp.float32
    )
    dpre = (dact * gelu_slope(pre)).astype(jnp.bfloat16)
    dnorm = (
        lax.dot_general(dpre, proj_in, (((1,), (1,)), ((), ())), preferred_element_type=jnp.float32)
        * norm_gain
    )
    dconv = inv * (
        dnorm
        - jnp.mean(dnorm, axis=-1, keepdims=True)
        - nhat * jnp.mean(dnorm * nhat, axis=-1, keepdims=True)
    )
    dconv = dconv.astype(jnp.bfloat16).reshape(fields.shape)
    dplanes = to_channels(dconv)
    dpadded = jnp.pad(dplanes.astype(jnp.float32), ((0, 0), (0, 0), (3, 3), (3, 3)))
    flipped = dw_kernel.reshape(local_ch, 7, 7)[:, ::-1, ::-1].reshape(local_ch, 49)
    interior = grouped_conv(dpadded, flipped)
    kernels = edge_kernels(dw_kernel)
    band = rims_of(dplanes)
    flat_width = local_ch * 3 * size
    strip_grad = edge_grads(band, kernels)
    strip_grad = jnp.where(mirror[:, :, None, None, None], strip_grad[..., ::-1], strip_grad)
    targets = jnp.arange(total_samples * 4, dtype=jnp.int32)
    onehot = (targets[:, None] == source.reshape(-1)[None, :]).astype(jnp.float32)
    spread = jnp.dot(
        onehot, strip_grad.reshape(slots * 4, flat_width), precision=lax.Precision.HIGHEST
    )
    spread = spread.reshape(total_samples, 4, local_ch, 3, size)
    owned = lax.psum_scatter(
        spread.astype(jnp.bfloat16), "face", scatter_dimension=0, tiled=True
    ).astype(jnp.float32)
    interior = interior.at[:, :, 0:3, :].add(owned[:, 0])
    interior = interior.at[:, :, size - 3 :, :].add(owned[:, 1][:, :, ::-1, :])
    interior = interior.at[:, :, :, 0:3].add(jnp.swapaxes(owned[:, 2], 2, 3))
    interior = interior.at[:, :, :, size - 3 :].add(jnp.swapaxes(owned[:, 3][:, :, ::-1, :], 2, 3))
    conv_grad = to_cells(interior.astype(jnp.bfloat16))
    field_grad = (cotangent.astype(jnp.float32) + conv_grad.astype(jnp.float32)).astype(
        jnp.bfloat16
    )
    return (section_out.reshape(fields.shape), field_grad)

DEPTH = 3
TAPS = 7
SUB = 8
LANES = 128
SIDE = 16


def load_taps(w, half, q):
    return [w[half, pl.ds(TAPS * p + q, 1), :] for p in range(TAPS)]


def plus(total, part):
    return part if total is None else total + part


def widen_rows(xs, at, ref, rows, lead):
    width = ref.shape[2]
    for half in range(ref.shape[3] // LANES):
        lanes = pl.ds(half * LANES, LANES)

        def one(row, carry):
            xs[half, at + row, pl.ds(lead, width), :] = ref[0, row, :, lanes].astype(jnp.float32)
            return carry

        if rows > DEPTH:
            lax.fori_loop(0, rows, one, 0)
        else:
            for row in range(rows):
                one(row, 0)


def clear_pads(xs, width):
    halves, rows = xs.shape[:2]
    for half in range(halves):
        xs[half, :, pl.ds(0, SUB), :] = jnp.zeros((rows, SUB, LANES), jnp.float32)
        xs[half, :, pl.ds(SUB + width, SUB), :] = jnp.zeros((rows, SUB, LANES), jnp.float32)


def conv_partial_kernel(x_ref, w_ref, out_ref, xs):
    rows, width, chans = x_ref.shape[1:]
    clear_pads(xs, width)
    widen_rows(xs, 0, x_ref, rows, SUB)
    wide = 2
    for half in range(chans // LANES):
        lanes = pl.ds(half * LANES, LANES)

        def one(block, carry):
            start = pl.multiple_of(block * (SUB * wide), SUB * wide)
            acc = [[None] * rows for _ in range(wide)]
            for q in range(TAPS):
                taps = load_taps(w_ref, half, q)
                for row in range(rows):
                    for b in range(wide):
                        x = xs[half, row, pl.ds(start + SUB * (b + 1) - DEPTH + q, SUB), :]
                        for p in range(TAPS):
                            i = row + DEPTH - p
                            if 0 <= i < rows:
                                acc[b][i] = plus(acc[b][i], x * taps[p])
            bias = w_ref[half, pl.ds(TAPS * TAPS, 1), :]
            for b in range(wide):
                for i in range(rows):
                    out_ref[0, i, pl.ds(start + SUB * b, SUB), lanes] = acc[b][i] + bias
            return carry

        lax.fori_loop(0, width // (SUB * wide), one, 0)


def row_parts(xh, w, half, col):
    head = [None] * DEPTH
    tail = [None] * DEPTH
    for q in range(TAPS):
        for h in range(DEPTH):
            up = xh[half, h, pl.ds(col + SUB - DEPTH + q, SUB), :]
            down = xh[half, DEPTH + h, pl.ds(col + SUB - DEPTH + q, SUB), :]
            for i in range(h + 1):
                head[i] = plus(head[i], up * w[half, pl.ds(TAPS * (h - i) + q, 1), :])
            for k in range(DEPTH - h):
                tail[k] = plus(tail[k], down * w[half, pl.ds(TAPS * (h + k + 4) + q, 1), :])
    return head, tail


def end_parts(xh, w, half, col, first):
    out = [None] * DEPTH
    for q in range(TAPS):
        for h in range(DEPTH):
            x = xh[half, jnp.where(first, h, 2 * DEPTH - 1 - h), pl.ds(col + SUB - DEPTH + q, SUB), :]
            for d in range(h + 1):
                p = jnp.where(first, h - d, TAPS - 1 - h + d)
                out[d] = plus(out[d], x * w[half, pl.ds(TAPS * p + q, 1), :])
    return out


def column_parts(xc, w, half, starts):
    rows = xc.shape[1] - 2 * DEPTH
    acc = [None] * rows
    for q, start in starts:
        taps = load_taps(w, half, q)
        for row in range(rows + 2 * DEPTH):
            x = xc[half, row, pl.ds(start, SUB), :]
            for p in range(TAPS):
                if 0 <= row - p < rows:
                    acc[row - p] = plus(acc[row - p], x * taps[p])
    return acc


def cells_of(cells, x, cot, vec, bias_in, w_in, w_out, w_out_t, w_in_t):
    chans = cells.shape[1]
    gain, shift, bias_out, scale = (vec[k : k + 1, :] for k in range(4))
    hidden = w_in.shape[1]
    piece = 256
    cells = cells.astype(jnp.bfloat16).astype(jnp.float32)
    mean = jnp.sum(cells, axis=-1, keepdims=True) * (1.0 / chans)
    centred = cells - mean
    inv = lax.rsqrt(jnp.sum(centred * centred, axis=-1, keepdims=True) * (1.0 / chans) + EPSILON)
    nhat = centred * inv
    normed = (nhat * gain + shift).astype(jnp.bfloat16)
    dmix = (scale * cot.astype(jnp.float32)).astype(jnp.bfloat16)
    mlp = None
    dnorm = None
    for first in range(0, hidden, piece):
        cut = pl.ds(first, piece)
        pre = jnp.dot(normed, w_in[:, cut], preferred_element_type=jnp.float32) + bias_in[0:1, cut]
        dact = jnp.dot(dmix, w_out_t[:, cut], preferred_element_type=jnp.float32)
        square = pre * pre
        tanh_val = jnp.tanh(pre * (GELU_SCALE + (GELU_SCALE * GELU_CUBIC) * square))
        lifted = 0.5 + 0.5 * tanh_val
        act = (pre * lifted).astype(jnp.bfloat16)
        bend = pre * ((0.5 * GELU_SCALE) + (1.5 * GELU_SCALE * GELU_CUBIC) * square)
        slope = lifted + (1.0 - tanh_val * tanh_val) * bend
        dpre = (dact * slope).astype(jnp.bfloat16)
        mlp = plus(mlp, jnp.dot(act, w_out[cut, :], preferred_element_type=jnp.float32))
        dnorm = plus(dnorm, jnp.dot(dpre, w_in_t[cut, :], preferred_element_type=jnp.float32))
    section = (x.astype(jnp.float32) + scale * (mlp + bias_out)).astype(jnp.bfloat16)
    dnorm = dnorm * gain
    first_mean = jnp.sum(dnorm, axis=-1, keepdims=True) * (1.0 / chans)
    second_mean = jnp.sum(dnorm * nhat, axis=-1, keepdims=True) * (1.0 / chans)
    dconv = (inv * (dnorm - first_mean - nhat * second_mean)).astype(jnp.bfloat16)
    return section, dconv


def edge_kernel(
    flags, cl, cr, ce, xl, xr, xe, gl, gr, ge, top, bot, left, right, w, wt, vec, bi, wi, wo, wot, wit,
    sl, sr, se, dl, dr, de, tb, xh, xcl, xcr, lrs, ends,
):
    rows, chans = cl.shape[1], cl.shape[3]
    width = top.shape[2]
    inner = width - 2 * SIDE
    mats = (vec, bi, wi, wo, wot, wit)
    first = flags[0] == 1
    clear_pads(xh, width)
    widen_rows(xh, 0, top, DEPTH, SUB)
    widen_rows(xh, DEPTH, bot, DEPTH, SUB)
    for half in range(chans // LANES):
        lanes = pl.ds(half * LANES, LANES)
        xcl[half, :, pl.ds(0, SUB), :] = left[0, :, :, lanes].astype(jnp.float32)
        xcl[half, :, pl.ds(SUB, SUB), :] = jnp.zeros((rows + 2 * DEPTH, SUB, LANES), jnp.float32)
        xcr[half, :, pl.ds(0, SUB), :] = jnp.zeros((rows + 2 * DEPTH, SUB, LANES), jnp.float32)
        xcr[half, :, pl.ds(SUB, SUB), :] = right[0, :, :, lanes].astype(jnp.float32)
    lrs[0] = cl[0]
    lrs[1] = cr[0]
    for half in range(chans // LANES):
        lanes = pl.ds(half * LANES, LANES)
        near = column_parts(xcl, w, half, [(q, SUB - DEPTH + q) for q in range(DEPTH)])
        far = column_parts(xcr, w, half, [(q, q - DEPTH) for q in range(4, TAPS)])
        for i in range(rows):
            lrs[0, i, pl.ds(0, SUB), lanes] += near[i]
            lrs[1, i, pl.ds(SIDE - SUB, SUB), lanes] += far[i]
        for side in range(2):
            for b in range(0, SIDE, SUB):
                head, tail = row_parts(xh, w, half, b + side * (width - SIDE))
                for d in range(DEPTH):
                    lrs[side, d, pl.ds(b, SUB), lanes] += head[d]
                    lrs[side, rows - 1 - d, pl.ds(b, SUB), lanes] += tail[d]
    flat = (2 * rows * SIDE, chans)
    both = lambda a, b: jnp.stack([a[0], b[0]]).reshape(flat)
    section, dconv = cells_of(lrs[...].reshape(flat), both(xl, xr), both(gl, gr), *mats)
    section = section.reshape(2, rows, SIDE, chans)
    dconv = dconv.reshape(2, rows, SIDE, chans)
    sl[0] = section[0]
    sr[0] = section[1]
    dl[0] = dconv[0]
    dr[0] = dconv[1]

    @pl.when(flags[0] + flags[1] > 0)
    def _():
        at = [jnp.where(first, d, SUB - 1 - d) for d in range(DEPTH)]
        whole_at = [jnp.where(first, d, rows - 1 - d) for d in range(DEPTH)]
        mid = pl.ds(SIDE, inner)
        for d in range(DEPTH):
            ends[d] = ce[0, at[d], mid, :]
        for half in range(chans // LANES):
            lanes = pl.ds(half * LANES, LANES)

            def one(block, carry):
                start = pl.multiple_of(block * SUB, SUB)
                parts = end_parts(xh, w, half, start + SIDE, first)
                for d in range(DEPTH):
                    ends[d, pl.ds(start, SUB), lanes] += parts[d]
                return carry

            lax.fori_loop(0, inner // SUB, one, 0)
        rim = lambda ref: jnp.stack([ref[0, at[d], mid, :] for d in range(DEPTH)]).reshape(DEPTH * inner, chans)
        section, dconv = cells_of(ends[...].reshape(DEPTH * inner, chans), rim(xe), rim(ge), *mats)
        se[0] = section.reshape(DEPTH, inner, chans)
        dconv = dconv.reshape(DEPTH, inner, chans)
        de[0] = dconv
        for half in range(chans // LANES):
            lanes = pl.ds(half * LANES, LANES)
            for d in range(DEPTH):
                xh[half, d, pl.ds(SUB, SIDE), :] = dl[0, whole_at[d], :, lanes].astype(jnp.float32)
                xh[half, d, pl.ds(SUB + SIDE, inner), :] = de[0, d, :, lanes].astype(jnp.float32)
                xh[half, d, pl.ds(SUB + SIDE + inner, SIDE), :] = dr[0, whole_at[d], :, lanes].astype(jnp.float32)

            def one_strip(block, carry):
                start = pl.multiple_of(block * SUB, SUB)
                out = [None] * DEPTH
                for q in range(TAPS):
                    for edge in range(DEPTH):
                        x = xh[half, edge, pl.ds(start + SUB - DEPTH + q, SUB), :]
                        for d in range(DEPTH - edge):
                            p = jnp.where(first, edge + d + 4, 2 - edge - d)
                            out[d] = plus(out[d], x * wt[half, pl.ds(TAPS * p + q, 1), :])
                for d in range(DEPTH):
                    xh[half, DEPTH + d, pl.ds(start + SUB, SUB), :] = out[d]
                return carry

            lax.fori_loop(0, width // SUB, one_strip, 0)
            for d in range(DEPTH):
                tb[0, d, :, lanes] = xh[half, DEPTH + d, pl.ds(SUB, width), :].astype(jnp.bfloat16)


def strip_kernel(left, right, wt, near_ref, far_ref, xcl, xcr):
    rows, chans = near_ref.shape[1], near_ref.shape[3]
    for half in range(chans // LANES):
        lanes = pl.ds(half * LANES, LANES)
        zeros = jnp.zeros((rows + 2 * DEPTH, SUB, LANES), jnp.float32)
        xcl[half, :, pl.ds(0, SUB), :] = zeros
        xcl[half, :, pl.ds(SUB, SUB), :] = left[0, :, :, lanes].astype(jnp.float32)
        xcr[half, :, pl.ds(0, SUB), :] = right[0, :, :, lanes].astype(jnp.float32)
        xcr[half, :, pl.ds(SUB, SUB), :] = zeros
    for half in range(chans // LANES):
        lanes = pl.ds(half * LANES, LANES)
        near = column_parts(xcl, wt, half, [(q, q - DEPTH) for q in range(4, TAPS)])
        far = column_parts(xcr, wt, half, [(q, SUB - DEPTH + q) for q in range(DEPTH)])
        for i in range(rows):
            near_ref[0, i, :, lanes] = near[i]
            far_ref[0, i, :, lanes] = far[i]


def interior_kernel(
    flags, conv, x, cot, top, bot, sl, sr, se, dl, dr, de, w, vec, bi, wi, wo, wot, wit, sec, dc, xh, cs
):
    rows, width, chans = conv.shape[1:]
    inner = width - 2 * SIDE
    mid = pl.ds(SIDE, inner)
    mats = (vec, bi, wi, wo, wot, wit)
    for full, near, far in ((sec, sl, sr), (dc, dl, dr)):
        full[0, :, pl.ds(0, SIDE), :] = near[0]
        full[0, :, pl.ds(width - SIDE, SIDE), :] = far[0]
    clear_pads(xh, width)
    widen_rows(xh, 0, top, DEPTH, SUB)
    widen_rows(xh, DEPTH, bot, DEPTH, SUB)
    last = rows - DEPTH
    cs[pl.ds(0, DEPTH)] = conv[0, pl.ds(0, DEPTH), mid, :]
    cs[pl.ds(DEPTH, DEPTH)] = conv[0, pl.ds(last, DEPTH), mid, :]
    for half in range(chans // LANES):
        lanes = pl.ds(half * LANES, LANES)

        def one(block, carry):
            start = pl.multiple_of(block * SUB, SUB)
            head, tail = row_parts(xh, w, half, start + SIDE)
            for d in range(DEPTH):
                cs[d, pl.ds(start, SUB), lanes] += head[d]
                cs[2 * DEPTH - 1 - d, pl.ds(start, SUB), lanes] += tail[d]
            return carry

        lax.fori_loop(0, inner // SUB, one, 0)

    at_end = flags[0] + flags[1] > 0

    @pl.when(jnp.logical_not(at_end))
    def _():
        flat = (2 * DEPTH * inner, chans)
        pick = lambda ref: jnp.concatenate([ref[0, pl.ds(0, DEPTH), mid, :], ref[0, pl.ds(last, DEPTH), mid, :]]).reshape(flat)
        section, dconv = cells_of(cs[...].reshape(flat), pick(x), pick(cot), *mats)
        for full, value in ((sec, section), (dc, dconv)):
            value = value.reshape(2 * DEPTH, inner, chans)
            full[0, pl.ds(0, DEPTH), mid, :] = value[:DEPTH]
            full[0, pl.ds(last, DEPTH), mid, :] = value[DEPTH:]

    @pl.when(at_end)
    def _():
        flat = (DEPTH * inner, chans)
        first = flags[0] == 1
        base = jnp.where(first, last, 0)
        rim = pl.ds(base, DEPTH)
        section, dconv = cells_of(
            cs[pl.ds(jnp.where(first, DEPTH, 0), DEPTH)].reshape(flat),
            x[0, rim, mid, :].reshape(flat),
            cot[0, rim, mid, :].reshape(flat),
            *mats,
        )
        for full, value, done in ((sec, section, se), (dc, dconv, de)):
            full[0, rim, mid, :] = value.reshape(DEPTH, inner, chans)
            for d in range(DEPTH):
                full[0, jnp.where(first, d, rows - 1 - d), mid, :] = done[0, d]

    free = rows - 2 * DEPTH
    step = free // 2

    def some(block, carry):
        flat = (step * inner, chans)
        these = pl.ds(DEPTH + block * step, step)
        section, dconv = cells_of(
            conv[0, these, mid, :].reshape(flat), x[0, these, mid, :].reshape(flat), cot[0, these, mid, :].reshape(flat), *mats
        )
        sec[0, these, mid, :] = section.reshape(step, inner, chans)
        dc[0, these, mid, :] = dconv.reshape(step, inner, chans)
        return carry

    lax.fori_loop(0, 2, some, 0)


def join_kernel(grad, cot, above, below, top, bot, left, right, wt, out, xh, total):
    rows, width, chans = grad.shape[1:]
    clear_pads(xh, width)
    widen_rows(xh, 0, above, DEPTH, SUB)
    widen_rows(xh, DEPTH, below, DEPTH, SUB)
    total[...] = grad[0]
    for half in range(chans // LANES):
        lanes = pl.ds(half * LANES, LANES)

        def one(block, carry):
            start = pl.multiple_of(block * SUB, SUB)
            head, tail = row_parts(xh, wt, half, start)
            for d in range(DEPTH):
                total[d, pl.ds(start, SUB), lanes] += head[d]
                total[rows - 1 - d, pl.ds(start, SUB), lanes] += tail[d]
            return carry

        lax.fori_loop(0, width // SUB, one, 0)
    total[pl.ds(0, DEPTH)] += top[0].astype(jnp.float32)
    total[pl.ds(rows - DEPTH, DEPTH)] += bot[0].astype(jnp.float32)
    total[:, pl.ds(0, SUB), :] += left[0].astype(jnp.float32)
    total[:, pl.ds(width - SUB, SUB), :] += right[0].astype(jnp.float32)

    def finish(row, carry):
        conv_grad = total[row].astype(jnp.bfloat16).astype(jnp.float32)
        out[0, row] = (cot[0, row].astype(jnp.float32) + conv_grad).astype(jnp.bfloat16)
        return carry

    lax.fori_loop(0, rows, finish, 0)


def by_slot(x, base=0):
    return pl.BlockSpec((1,) + tuple(x.shape[1:]), lambda s, *_: (s + base if base else s,) + (0,) * (len(x.shape) - 1))


def whole(x):
    return pl.BlockSpec(tuple(x.shape), lambda s, *_: (0,) * len(x.shape))


def run(kernel, name, span, ins, specs, outs, scratch, flags=None, micros=10, into=()):
    base, slots = span
    prefetch = () if flags is None else (flags,)
    first = len(prefetch) + len(ins)

    def body(*refs):
        return kernel(*refs[:first], *refs[first + len(into) :])

    return pl.pallas_call(
        body,
        grid_spec=pltpu.PrefetchScalarGridSpec(
            num_scalar_prefetch=len(prefetch),
            grid=(slots,),
            in_specs=specs + [pl.BlockSpec(memory_space=pl.ANY)] * len(into),
            out_specs=[by_slot(o, base) for o in outs],
            scratch_shapes=[pltpu.VMEM(s, jnp.float32) for s in scratch],
        ),
        out_shape=list(outs),
        input_output_aliases={first + k: k for k in range(len(into))},
        compiler_params=pltpu.CompilerParams(vmem_limit_bytes=60 * 1024 * 1024),
        cost_estimate=pl.CostEstimate(
            flops=micros * 1_000_000_000, transcendentals=0, bytes_accessed=sum(o.size * 2 for o in outs)
        ),
        name=name,
    )(*prefetch, *ins, *into)


def conv_partial(x, weights, name, span, into=()):
    slots, rows, width, chans = x.shape
    out = jax.ShapeDtypeStruct(x.shape, jnp.float32)
    pads = (chans // LANES, rows, width + 2 * SUB, LANES)
    specs = [by_slot(x, span[0]), whole(weights)]
    return run(conv_partial_kernel, name, span, (x, weights), specs, [out], [pads], micros=9 * span[1], into=into)[0]


def face_all(own):
    groups = lax.axis_size("face")
    send = jnp.broadcast_to(own[None], (groups,) + own.shape)
    return lax.all_to_all(send, "face", split_axis=0, concat_axis=0, tiled=True)


def turn_sides(sides, flip):
    tiles = lax.axis_size("tile")
    mirrored = lax.ppermute(sides, "tile", [(t, tiles - 1 - t) for t in range(tiles)])
    return jnp.where(flip[:, :, None, None, None], mirrored[:, :, :, ::-1], sides)


def turn_ends(ends, flip):
    here = jnp.where(lax.axis_index("tile") == 0, flip[:, 0], flip[:, 1])
    return jnp.where(here[:, None, None, None], ends[:, :, ::-1], ends)


def to_neighbours(head, tail):
    tiles, chans = lax.axis_size("tile"), head.shape[-1]
    after = jnp.arange(tiles, dtype=jnp.int32) == lax.axis_index("tile") + 1
    rows = jnp.where(after[:, None, None], tail.reshape(1, -1, chans), head.reshape(1, -1, chans))
    return jnp.pad(rows, ((0, 0), (0, -rows.shape[1] % 8), (0, 0)))


def from_neighbours(got, shape):
    tiles, tile = lax.axis_size("tile"), lax.axis_index("tile")
    count = 1
    for extent in shape[:-1]:
        count *= extent
    above = lax.dynamic_index_in_dim(got, jnp.maximum(tile - 1, 0), 0, False)[:count].reshape(shape)
    below = lax.dynamic_index_in_dim(got, jnp.minimum(tile + 1, tiles - 1), 0, False)[:count].reshape(shape)
    return jnp.where(tile == 0, 0, above), jnp.where(tile == tiles - 1, 0, below)


def spread_ends(ends, rider):
    slots, _, width, chans = ends.shape
    tiles = lax.axis_size("tile")
    rows = width // tiles
    send = jnp.moveaxis(ends.reshape(slots, DEPTH, tiles, rows, chans), 2, 0).reshape(tiles, -1, chans)
    send = jnp.concatenate([send, rider], axis=1)
    got = lax.all_to_all(send, "tile", split_axis=0, concat_axis=0, tiled=True)
    count = slots * DEPTH * rows
    found = jnp.stack([got[0, :count], got[tiles - 1, :count]]).reshape(2, slots, DEPTH, rows, chans)
    return jnp.moveaxis(found, 0, 1), got[:, count:]


def in_three(values):
    parts = []
    for _ in range(3):
        part = lax.reduce_precision(values, 8, 7)
        parts.append(part.astype(jnp.bfloat16))
        values = values - part
    return jnp.stack(parts)


def pick(found, index):
    groups, slots, _, _, rows, chans = found.shape
    strips = found.reshape(groups * slots * 4, DEPTH, rows, chans)
    return jnp.take(strips, index.reshape(-1), axis=0).reshape(slots, 4, DEPTH, rows, chans)


def gather_ends(found, rider=None):
    slots, _, _, rows, chans = found.shape
    tiles = lax.axis_size("tile")
    half = tiles // 2
    send = jnp.stack([found[:, 0]] * half + [found[:, 1]] * (tiles - half)).reshape(tiles, -1, chans)
    count = send.shape[1]
    if rider is not None:
        send = jnp.concatenate([send, rider], axis=1)
    got = lax.all_to_all(send, "tile", split_axis=0, concat_axis=0, tiled=True)
    ends = got[:, :count].reshape(tiles, slots, DEPTH, rows, chans)
    return jnp.moveaxis(ends, 0, 2).reshape(slots, DEPTH, tiles * rows, chans), got[:, count:]


def halo(first, last):
    tiles = lax.axis_size("tile")
    above = lax.ppermute(last, "tile", [(t, t + 1) for t in range(tiles - 1)])
    below = lax.ppermute(first, "tile", [(t + 1, t) for t in range(tiles - 1)])
    return above, below


def row_shards(
    fields,
    cotangent,
    dw_kernel,
    dw_bias,
    norm_gain,
    norm_bias,
    proj_in,
    bias_in,
    proj_out,
    bias_out,
    layer_scale,
    strip_source,
    strip_flip,
):
    slots, rows, width, chans = fields.shape
    tiles = lax.axis_size("tile")
    tile = lax.axis_index("tile")
    first_tile, last_tile = tile == 0, tile == tiles - 1
    flags = jnp.stack([first_tile, last_tile]).astype(jnp.int32)
    own_samples = lax.axis_index("face") * slots + jnp.arange(slots, dtype=jnp.int32)
    source, mirror = reader_tables(own_samples, strip_source, strip_flip)
    entries = jnp.arange(48, dtype=jnp.int32)
    hits = strip_source[None, :] == entries[:, None]
    reader_of = jnp.sum(jnp.where(hits, entries[None, :], 0), axis=1)
    flip_of = jnp.sum(jnp.where(hits, strip_flip[None, :], 0), axis=1)
    own_strips = (own_samples % 12)[:, None] * 4 + jnp.arange(4, dtype=jnp.int32)[None, :]
    target = (own_samples // 12)[:, None] * 48 + reader_of[own_strips]
    target_mirror = flip_of[own_strips] == 1

    own_taps = jnp.concatenate([dw_kernel, dw_bias[:, None]], axis=1).T
    own_chans = own_taps.shape[1]
    taps_count = TAPS * TAPS + 1
    rider_rows = -(-3 * taps_count * own_chans // chans)
    rider_rows += -rider_rows % 8
    rider = in_three(own_taps).reshape(-1)
    rider = jnp.pad(rider, (0, rider_rows * chans - rider.size)).reshape(rider_rows, chans)
    ends = jnp.where(first_tile, fields[:, :DEPTH], fields[:, : rows - DEPTH - 1 : -1])
    ends = turn_ends(ends, target_mirror[:, :2])
    near_ends, riders = spread_ends(ends, jnp.broadcast_to(rider[None], (tiles,) + rider.shape))
    riders = riders.reshape(tiles, -1)[:, : 3 * taps_count * own_chans].astype(jnp.float32)
    riders = riders.reshape(tiles, 3, taps_count, own_chans)
    taps = (riders[:, 0] + riders[:, 1]) + riders[:, 2]
    taps = jnp.moveaxis(taps, 0, 1).reshape(taps_count, chans)
    taps = jnp.pad(taps, ((0, 6), (0, 0)))
    weights = jnp.moveaxis(taps.reshape(-1, chans // LANES, LANES), 1, 0)
    turned = jnp.pad(weights[:, TAPS * TAPS - 1 :: -1], ((0, 0), (0, 7), (0, 0)))
    vectors = jnp.stack([norm_gain, norm_bias, bias_out, layer_scale])
    mats = (vectors, bias_in[None], proj_in, proj_out, proj_out.T, proj_in.T)

    side_pair = jnp.stack([fields[:, :, :DEPTH], fields[:, :, : width - DEPTH - 1 : -1]], axis=1)
    sides = turn_sides(jnp.swapaxes(side_pair, 2, 3), target_mirror[:, 2:])
    own = jnp.concatenate([near_ends, sides], axis=1)
    found = face_all(own)
    early, own = lax.optimization_barrier((fields, own))
    above, below = halo(early[:, :DEPTH], early[:, rows - DEPTH :])
    partial = conv_partial(early, weights, "conv_partial", (0, 2))
    partial, found, above, below = lax.optimization_barrier((partial, found, above, below))
    picked = pick(found, source)
    late, picked = lax.optimization_barrier((fields, picked))
    sides = picked[:, 2:]
    rider = to_neighbours(sides[:, :, :, :DEPTH], sides[:, :, :, rows - DEPTH :])
    new_ends, riders = gather_ends(picked[:, :2], rider)
    side_above, side_below = from_neighbours(riders, (slots, 2, DEPTH, DEPTH, chans))
    sides = jnp.concatenate([side_above, sides, side_below], axis=3)
    partial = conv_partial(late, weights, "conv_partial_rest", (2, slots - 2), (partial,))
    sides = jnp.swapaxes(sides, 2, 3)
    left = jnp.pad(sides[:, 0, :, ::-1], ((0, 0), (0, 0), (SUB - DEPTH, 0), (0, 0)))
    right = jnp.pad(sides[:, 1], ((0, 0), (0, 0), (0, SUB - DEPTH), (0, 0)))
    top = jnp.where(first_tile, new_ends[:, ::-1], above)
    bot = jnp.where(last_tile, new_ends, below)

    near_spec = pl.BlockSpec((1, rows, SIDE, chans), lambda s, f: (s, 0, 0, 0))
    far_spec = pl.BlockSpec((1, rows, SIDE, chans), lambda s, f: (s, 0, width // SIDE - 1, 0))
    end_spec = pl.BlockSpec((1, SUB, width, chans), lambda s, f: (s, f[1] * (rows // SUB - 1), 0, 0))
    side_out = jax.ShapeDtypeStruct((slots, rows, SIDE, chans), jnp.bfloat16)
    end_out = jax.ShapeDtypeStruct((slots, DEPTH, width - 2 * SIDE, chans), jnp.bfloat16)
    strip_out = jax.ShapeDtypeStruct((slots, DEPTH, width, chans), jnp.bfloat16)
    halves = chans // LANES
    halo_pads = (halves, 2 * DEPTH, width + 2 * SUB, LANES)
    side_pads = (halves, rows + 2 * DEPTH, 2 * SUB, LANES)
    extras = (top, bot, left, right)
    sl, sr, se, dl, dr, de, tb = run(
        edge_kernel,
        "edge_cells",
        (0, slots),
        (partial,) * 3 + (fields,) * 3 + (cotangent,) * 3 + extras + (weights, turned) + mats,
        [near_spec, far_spec, end_spec] * 3 + [by_slot(x) for x in extras] + [whole(x) for x in (weights, turned) + mats],
        [side_out, side_out, end_out, side_out, side_out, end_out, strip_out],
        [halo_pads, side_pads, side_pads, (2, rows, SIDE, chans), (DEPTH, width - 2 * SIDE, chans)],
        flags,
        micros=23,
    )

    outer = jnp.stack([dl[:, :, :SUB], dr[:, :, SIDE - SUB :]], axis=1)
    rims = jnp.stack([outer[:, 0, :, :DEPTH], outer[:, 1, :, SUB - DEPTH :]], axis=1)
    near_ends, riders = spread_ends(tb, to_neighbours(rims[:, :, :DEPTH], rims[:, :, rows - DEPTH :]))
    shown = []
    for rim in from_neighbours(riders, (slots, 2, DEPTH, DEPTH, chans)):
        blank = jnp.zeros((slots, DEPTH, SUB - DEPTH, chans), rim.dtype)
        shown.append(
            jnp.stack([jnp.concatenate([rim[:, 0], blank], axis=2), jnp.concatenate([blank, rim[:, 1]], axis=2)], axis=1)
        )
    outer = jnp.concatenate([shown[0], outer, shown[1]], axis=2)
    strip = jax.ShapeDtypeStruct((slots, rows, SUB, chans), jnp.float32)
    ins = (outer[:, 0], outer[:, 1])
    near, far = run(
        strip_kernel,
        "side_strips",
        (0, slots),
        ins + (turned,),
        [by_slot(x) for x in ins] + [whole(turned)],
        [strip, strip],
        [side_pads, side_pads],
    )
    side_pair = jnp.stack([near[:, :, : SUB - DEPTH - 1 : -1], far[:, :, :DEPTH]], axis=1).astype(jnp.bfloat16)
    own = jnp.concatenate([near_ends, jnp.swapaxes(side_pair, 2, 3)], axis=1)
    found = face_all(own)

    full = jax.ShapeDtypeStruct(fields.shape, jnp.bfloat16)
    ins = (partial, fields, cotangent, top, bot, sl, sr, se, dl, dr, de)
    done = ()
    for span, sign in (((0, 1), tb), ((1, slots - 1), own)):
        gated = lax.optimization_barrier((fields, sign))[0]
        ins = (partial, gated, cotangent, top, bot, sl, sr, se, dl, dr, de)
        done = run(
            interior_kernel,
            "interior_cells",
            span,
            ins + (weights,) + mats,
            [by_slot(x, span[0]) for x in ins] + [whole(x) for x in (weights,) + mats],
            [full, full],
            [halo_pads, (2 * DEPTH, width - 2 * SIDE, chans)],
            flags,
            micros=10 * span[1],
            into=done,
        )
    section_out, dconv = done
    above, below = halo(dconv[:, :DEPTH], dconv[:, rows - DEPTH :])
    grad = conv_partial(dconv, turned, "conv_gradient", (0, 1))
    grad, found = lax.optimization_barrier((grad, found))
    picked = pick(found, target)
    late, picked = lax.optimization_barrier((dconv, picked))
    sides = turn_sides(picked[:, 2:], target_mirror[:, 2:])
    ends = turn_ends(gather_ends(picked[:, :2])[0], target_mirror[:, :2])
    grad = conv_partial(late, turned, "conv_gradient_rest", (1, slots - 1), (grad,))

    top = jnp.where(first_tile, ends, 0)
    bot = jnp.where(last_tile, ends[:, ::-1], 0)
    sides = jnp.swapaxes(sides, 2, 3)
    left = jnp.pad(sides[:, 0], ((0, 0), (0, 0), (0, SUB - DEPTH), (0, 0)))
    right = jnp.pad(sides[:, 1, :, ::-1], ((0, 0), (0, 0), (SUB - DEPTH, 0), (0, 0)))
    ins = (grad, cotangent, above, below, top, bot, left, right)
    field_grad = run(
        join_kernel,
        "join",
        (0, slots),
        ins + (turned,),
        [by_slot(x) for x in ins] + [whole(turned)],
        [full],
        [halo_pads, (rows, width, chans)],
    )[0]
    return (section_out, field_grad)


def block_of(fields, *rest):
    rows, width, chans = fields.shape[1:]
    if rows % SUB == 0 and rows <= 16 and chans % LANES == 0 and width % SIDE == 0 and width > 4 * SIDE:
        return row_shards(fields, *rest)
    return shards(fields, *rest)


def solution(mesh):
    placed = (
        P("face", "tile", None, None),
        P("face", "tile", None, None),
        P("tile", None),
        P("tile"),
        P(),
        P(),
        P(),
        P(),
        P(),
        P(),
        P(),
        P(),
        P(),
    )
    return jax.shard_map(
        block_of,
        mesh=mesh,
        in_specs=placed,
        out_specs=(P("face", "tile", None, None), P("face", "tile", None, None)),
        check_vma=False,
    )
```

```python
import jax
import jax.numpy as jnp
from jax import lax
from jax.experimental import pallas as pl
from jax.experimental.pallas import tpu as pltpu
from jax.sharding import PartitionSpec as P

EPSILON = 1e-06
GELU_SCALE = 0.7978845608028654
GELU_CUBIC = 0.044715


def gelu_value(pre):
    inner = GELU_SCALE * (pre + GELU_CUBIC * pre * pre * pre)
    return 0.5 * pre * (1.0 + jnp.tanh(inner))


def gelu_slope(pre):
    tanh_val = jnp.tanh(GELU_SCALE * (pre + GELU_CUBIC * pre * pre * pre))
    return 0.5 * (1.0 + tanh_val) + 0.5 * pre * (1.0 - tanh_val * tanh_val) * GELU_SCALE * (
        1.0 + 3.0 * GELU_CUBIC * pre * pre
    )


def to_channels(cells):
    turned = jnp.transpose(cells, (0, 3, 1, 2))
    return lax.all_to_all(turned, "tile", split_axis=1, concat_axis=2, tiled=True)


def to_cells(planes):
    moved = lax.all_to_all(planes, "tile", split_axis=2, concat_axis=1, tiled=True)
    return jnp.transpose(moved, (0, 2, 3, 1))


def rims_of(planes):
    top = planes[:, :, 0:3, :]
    bottom = planes[:, :, ::-1, :][:, :, 0:3, :]
    left = jnp.swapaxes(planes[:, :, :, 0:3], 2, 3)
    right = jnp.swapaxes(planes[:, :, :, ::-1][:, :, :, 0:3], 2, 3)
    return jnp.stack([top, bottom, left, right], axis=1)


def edge_kernels(taps):
    kernel = taps.reshape(taps.shape[0], 7, 7)
    swapped = jnp.swapaxes(kernel, 1, 2)
    return jnp.stack([kernel, kernel[:, ::-1, :], swapped, swapped[:, ::-1, :]])


def edge_grads(band, kernels):
    size = band.shape[-1]
    padded = jnp.pad(band.astype(jnp.float32), ((0, 0), (0, 0), (0, 0), (0, 0), (3, 3)))
    layers = []
    for depth in range(3):
        total = jnp.zeros(band.shape[:3] + (size,), jnp.float32)
        for inner in range(3 - depth):
            for along in range(7):
                weight = kernels[:, :, 2 - depth - inner, along][None, :, :, None]
                total = total + weight * padded[:, :, :, inner, 6 - along : 6 - along + size]
        layers.append(total)
    return jnp.stack(layers, axis=3)


def grouped_conv(planes_wide, taps):
    chans = taps.shape[0]
    return lax.conv_general_dilated(
        planes_wide,
        taps.reshape(chans, 1, 7, 7),
        (1, 1),
        "VALID",
        dimension_numbers=("NCHW", "OIHW", "NCHW"),
        feature_group_count=chans,
        precision=lax.Precision.HIGHEST,
    )


def reader_tables(sample, strip_source, strip_flip):
    reader = (sample % 12)[:, None] * 4 + jnp.arange(4, dtype=jnp.int32)[None, :]
    source = (sample // 12)[:, None] * 48 + strip_source[reader]
    return (source, strip_flip[reader] == 1)


def shards(
    fields,
    cotangent,
    dw_kernel,
    dw_bias,
    norm_gain,
    norm_bias,
    proj_in,
    bias_in,
    proj_out,
    bias_out,
    layer_scale,
    strip_source,
    strip_flip,
):
    slots = fields.shape[0]
    size = fields.shape[2]
    chans = fields.shape[3]
    total_samples = slots * lax.axis_size("face")
    first = lax.axis_index("face") * slots
    own_samples = first + jnp.arange(slots, dtype=jnp.int32)
    source, mirror = reader_tables(own_samples, strip_source, strip_flip)
    planes = to_channels(fields)
    local_ch = planes.shape[1]
    all_rims = lax.all_gather(rims_of(planes), "face", axis=0, tiled=True)
    picked = jnp.take(
        all_rims.reshape(total_samples * 4, local_ch, 3, size), source.reshape(-1), axis=0
    )
    picked = picked.reshape(slots, 4, local_ch, 3, size)
    strips = jnp.where(mirror[:, :, None, None, None], picked[..., ::-1], picked)
    left = jnp.swapaxes(strips[:, 2][:, :, ::-1, :], 2, 3)
    right = jnp.swapaxes(strips[:, 3], 2, 3)
    middle = jnp.concatenate([left, planes, right], axis=3)
    edge_pad = ((0, 0), (0, 0), (0, 0), (3, 3))
    top = jnp.pad(strips[:, 0][:, :, ::-1, :], edge_pad)
    bottom = jnp.pad(strips[:, 1], edge_pad)
    padded = jnp.concatenate([top, middle, bottom], axis=2)
    conv_sum = grouped_conv(padded.astype(jnp.float32), dw_kernel) + dw_bias[None, :, None, None]
    conv = to_cells(conv_sum.astype(jnp.bfloat16))
    cells = conv.reshape(-1, chans).astype(jnp.float32)
    mean = jnp.mean(cells, axis=-1, keepdims=True)
    centred = cells - mean
    inv = lax.rsqrt(jnp.mean(centred * centred, axis=-1, keepdims=True) + EPSILON)
    nhat = centred * inv
    normed = (nhat * norm_gain + norm_bias).astype(jnp.bfloat16)
    pre = jnp.dot(normed, proj_in, preferred_element_type=jnp.float32) + bias_in
    act = gelu_value(pre).astype(jnp.bfloat16)
    mlp = jnp.dot(act, proj_out, preferred_element_type=jnp.float32) + bias_out
    section_out = (fields.reshape(-1, chans).astype(jnp.float32) + layer_scale * mlp).astype(
        jnp.bfloat16
    )
    dmix = (layer_scale * cotangent.reshape(-1, chans).astype(jnp.float32)).astype(jnp.bfloat16)
    dact = lax.dot_general(
        dmix, proj_out, (((1,), (1,)), ((), ())), preferred_element_type=jnp.float32
    )
    dpre = (dact * gelu_slope(pre)).astype(jnp.bfloat16)
    dnorm = (
        lax.dot_general(dpre, proj_in, (((1,), (1,)), ((), ())), preferred_element_type=jnp.float32)
        * norm_gain
    )
    dconv = inv * (
        dnorm
        - jnp.mean(dnorm, axis=-1, keepdims=True)
        - nhat * jnp.mean(dnorm * nhat, axis=-1, keepdims=True)
    )
    dconv = dconv.astype(jnp.bfloat16).reshape(fields.shape)
    dplanes = to_channels(dconv)
    dpadded = jnp.pad(dplanes.astype(jnp.float32), ((0, 0), (0, 0), (3, 3), (3, 3)))
    flipped = dw_kernel.reshape(local_ch, 7, 7)[:, ::-1, ::-1].reshape(local_ch, 49)
    interior = grouped_conv(dpadded, flipped)
    kernels = edge_kernels(dw_kernel)
    band = rims_of(dplanes)
    flat_width = local_ch * 3 * size
    strip_grad = edge_grads(band, kernels)
    strip_grad = jnp.where(mirror[:, :, None, None, None], strip_grad[..., ::-1], strip_grad)
    targets = jnp.arange(total_samples * 4, dtype=jnp.int32)
    onehot = (targets[:, None] == source.reshape(-1)[None, :]).astype(jnp.float32)
    spread = jnp.dot(
        onehot, strip_grad.reshape(slots * 4, flat_width), precision=lax.Precision.HIGHEST
    )
    spread = spread.reshape(total_samples, 4, local_ch, 3, size)
    owned = lax.psum_scatter(
        spread.astype(jnp.bfloat16), "face", scatter_dimension=0, tiled=True
    ).astype(jnp.float32)
    interior = interior.at[:, :, 0:3, :].add(owned[:, 0])
    interior = interior.at[:, :, size - 3 :, :].add(owned[:, 1][:, :, ::-1, :])
    interior = interior.at[:, :, :, 0:3].add(jnp.swapaxes(owned[:, 2], 2, 3))
    interior = interior.at[:, :, :, size - 3 :].add(jnp.swapaxes(owned[:, 3][:, :, ::-1, :], 2, 3))
    conv_grad = to_cells(interior.astype(jnp.bfloat16))
    field_grad = (cotangent.astype(jnp.float32) + conv_grad.astype(jnp.float32)).astype(
        jnp.bfloat16
    )
    return (section_out.reshape(fields.shape), field_grad)

DEPTH = 3
TAPS = 7
SUB = 8
LANES = 128
SIDE = 16


def load_taps(w, half, q):
    return [w[half, pl.ds(TAPS * p + q, 1), :] for p in range(TAPS)]


def plus(total, part):
    return part if total is None else total + part


def widen_rows(xs, at, ref, rows, lead):
    width = ref.shape[2]
    for half in range(ref.shape[3] // LANES):
        lanes = pl.ds(half * LANES, LANES)

        def one(row, carry):
            xs[half, at + row, pl.ds(lead, width), :] = ref[0, row, :, lanes].astype(jnp.float32)
            return carry

        if rows > DEPTH:
            lax.fori_loop(0, rows, one, 0)
        else:
            for row in range(rows):
                one(row, 0)


def clear_pads(xs, width):
    halves, rows = xs.shape[:2]
    for half in range(halves):
        xs[half, :, pl.ds(0, SUB), :] = jnp.zeros((rows, SUB, LANES), jnp.float32)
        xs[half, :, pl.ds(SUB + width, SUB), :] = jnp.zeros((rows, SUB, LANES), jnp.float32)


EVEN = (TAPS + 1) // 2
ODD = TAPS // 2
SHARED = 2 * EVEN + ODD


def shared_taps(taps):
    chans = taps.shape[1]
    kernel = taps[: TAPS * TAPS].reshape(TAPS, TAPS, chans)
    even, odd = kernel[0::2], kernel[1::2]
    both = even + jnp.pad(odd, ((0, EVEN - ODD), (0, 0), (0, 0)))
    rows = jnp.moveaxis(jnp.concatenate([both, even, odd]), 0, 1).reshape(TAPS * SHARED, chans)
    rows = jnp.concatenate([rows, taps[TAPS * TAPS :]])
    rows = jnp.pad(rows, ((0, -rows.shape[0] % SUB), (0, 0)))
    return jnp.moveaxis(rows.reshape(-1, chans // LANES, LANES), 1, 0)


def conv_partial_kernel(x_ref, w_ref, out_ref, xs):
    rows, width, chans = x_ref.shape[1:]
    pairs = rows // 2
    before, after = pairs, 2 * pairs + 1
    mid = pl.ds(SUB, width)
    clear_pads(xs, width)
    for half in range(chans // LANES):
        lanes = pl.ds(half * LANES, LANES)

        def upper(k, carry):
            o = x_ref[0, 2 * k, :, lanes].astype(jnp.float32)
            xs[half, k, mid, :] = o
            xs[half, after + k, mid, :] = x_ref[0, 2 * k + 1, :, lanes].astype(jnp.float32) - o
            return carry

        def lower(k, carry):
            xs[half, before + k, mid, :] = x_ref[0, 2 * k - 1, :, lanes].astype(jnp.float32) - xs[half, k, mid, :]
            return carry

        lax.fori_loop(0, pairs, upper, 0)
        xs[half, before, mid, :] = -xs[half, 0, mid, :]
        lax.fori_loop(1, pairs, lower, 0)
        xs[half, before + pairs, mid, :] = x_ref[0, rows - 1, :, lanes].astype(jnp.float32)
    groups = ((0, pairs, 0, EVEN), (before, pairs + 1, EVEN, EVEN), (after, pairs, 2 * EVEN, ODD))
    wide = 2
    for half in range(chans // LANES):
        lanes = pl.ds(half * LANES, LANES)

        def one(block, carry):
            start = pl.multiple_of(block * (SUB * wide), SUB * wide)
            acc = [[[None] * pairs for _ in groups] for _ in range(wide)]
            for q in range(TAPS):
                for kind, (first, count, tap, many) in enumerate(groups):
                    taps = [w_ref[half, pl.ds(SHARED * q + tap + b, 1), :] for b in range(many)]
                    for row in range(count):
                        for part in range(wide):
                            x = xs[half, first + row, pl.ds(start + SUB * (part + 1) - DEPTH + q, SUB), :]
                            sums = acc[part][kind]
                            for b in range(many):
                                a = row + 1 - b
                                if 0 <= a < pairs:
                                    sums[a] = plus(sums[a], x * taps[b])
            bias = w_ref[half, pl.ds(SHARED * TAPS, 1), :]
            for part in range(wide):
                at = pl.ds(start + SUB * part, SUB)
                for a in range(pairs):
                    base = acc[part][0][a] + bias
                    out_ref[0, 2 * a, at, lanes] = base + acc[part][1][a]
                    out_ref[0, 2 * a + 1, at, lanes] = base + acc[part][2][a]
            return carry

        lax.fori_loop(0, width // (SUB * wide), one, 0)


def row_parts(xh, w, half, col):
    head = [None] * DEPTH
    tail = [None] * DEPTH
    for q in range(TAPS):
        for h in range(DEPTH):
            up = xh[half, h, pl.ds(col + SUB - DEPTH + q, SUB), :]
            down = xh[half, DEPTH + h, pl.ds(col + SUB - DEPTH + q, SUB), :]
            for i in range(h + 1):
                head[i] = plus(head[i], up * w[half, pl.ds(TAPS * (h - i) + q, 1), :])
            for k in range(DEPTH - h):
                tail[k] = plus(tail[k], down * w[half, pl.ds(TAPS * (h + k + 4) + q, 1), :])
    return head, tail


def end_parts(xe, w, half, col):
    out = [None] * DEPTH
    for q in range(TAPS):
        for h in range(DEPTH):
            x = xe[half, h, pl.ds(col + SUB - DEPTH + q, SUB), :]
            for d in range(h + 1):
                out[d] = plus(out[d], x * w[half, pl.ds(TAPS * (h - d) + q, 1), :])
    return out


def column_parts(xc, w, half, starts):
    rows = xc.shape[1] - 2 * DEPTH
    acc = [None] * rows
    for q, start in starts:
        taps = load_taps(w, half, q)
        for row in range(rows + 2 * DEPTH):
            x = xc[half, row, pl.ds(start, SUB), :]
            for p in range(TAPS):
                if 0 <= row - p < rows:
                    acc[row - p] = plus(acc[row - p], x * taps[p])
    return acc


def cells_of(cells, x, cot, vec, bias_in, w_in, w_out, w_out_t, w_in_t, acts, dpres):
    count, chans = cells.shape
    gain, shift, bias_twice, scale_half, scale, gain_half = (vec[k : k + 1, :] for k in range(6))
    hidden = w_in.shape[1]
    piece = 256
    here = pl.ds(0, count)
    cells = cells.astype(jnp.bfloat16).astype(jnp.float32)
    mean = jnp.sum(cells, axis=-1, keepdims=True) * (1.0 / chans)
    centred = cells - mean
    inv = lax.rsqrt(jnp.sum(centred * centred, axis=-1, keepdims=True) * (1.0 / chans) + EPSILON)
    nhat = centred * inv
    normed = (nhat * gain + shift).astype(jnp.bfloat16)
    dmix = (scale * cot.astype(jnp.float32)).astype(jnp.bfloat16)
    for first in range(0, hidden, piece):
        cut = pl.ds(first, piece)
        pre = jnp.dot(normed, w_in[:, cut], preferred_element_type=jnp.float32) + bias_in[0:1, cut]
        dact = jnp.dot(dmix, w_out_t[:, cut], preferred_element_type=jnp.float32)
        square = pre * pre
        tanh_val = jnp.tanh(pre * (GELU_SCALE + (GELU_SCALE * GELU_CUBIC) * square))
        lifted = 1.0 + tanh_val
        bend = pre * (GELU_SCALE + (3.0 * GELU_SCALE * GELU_CUBIC) * square)
        acts[here, cut] = (pre * lifted).astype(jnp.bfloat16)
        dpres[here, cut] = (dact * (lifted * (1.0 + (1.0 - tanh_val) * bend))).astype(jnp.bfloat16)
    mlp = jnp.dot(acts[here, :], w_out[...], preferred_element_type=jnp.float32)
    dnorm = jnp.dot(dpres[here, :], w_in_t[...], preferred_element_type=jnp.float32) * gain_half
    section = (x.astype(jnp.float32) + scale_half * (mlp + bias_twice)).astype(jnp.bfloat16)
    first_mean = jnp.sum(dnorm, axis=-1, keepdims=True) * (1.0 / chans)
    second_mean = jnp.sum(dnorm * nhat, axis=-1, keepdims=True) * (1.0 / chans)
    dconv = (inv * (dnorm - first_mean - nhat * second_mean)).astype(jnp.bfloat16)
    return section, dconv


def edge_kernel(
    flags, cl, cr, ce, xl, xr, xe, gl, gr, ge, top, bot, left, right, strip, w, wt, vec, bi, wi, wo, wot, wit,
    sl, sr, dl, dr, tb, xh, xcl, xcr, lrs, ends, we, wte, dends, acts, dpres,
):
    rows, chans = cl.shape[1], cl.shape[3]
    width = top.shape[2]
    inner = width - 2 * SIDE
    mats = (vec, bi, wi, wo, wot, wit, acts, dpres)
    first = flags[0] == 1
    clear_pads(xh, width)
    widen_rows(xh, 0, top, DEPTH, SUB)
    widen_rows(xh, DEPTH, bot, DEPTH, SUB)
    for half in range(chans // LANES):
        lanes = pl.ds(half * LANES, LANES)
        xcl[half, :, pl.ds(0, SUB), :] = left[0, :, :, lanes].astype(jnp.float32)
        xcl[half, :, pl.ds(SUB, SUB), :] = jnp.zeros((rows + 2 * DEPTH, SUB, LANES), jnp.float32)
        xcr[half, :, pl.ds(0, SUB), :] = jnp.zeros((rows + 2 * DEPTH, SUB, LANES), jnp.float32)
        xcr[half, :, pl.ds(SUB, SUB), :] = right[0, :, :, lanes].astype(jnp.float32)
    lrs[0] = cl[0]
    lrs[1] = cr[0]
    for half in range(chans // LANES):
        lanes = pl.ds(half * LANES, LANES)
        near = column_parts(xcl, w, half, [(q, SUB - DEPTH + q) for q in range(DEPTH)])
        far = column_parts(xcr, w, half, [(q, q - DEPTH) for q in range(4, TAPS)])
        for i in range(rows):
            lrs[0, i, pl.ds(0, SUB), lanes] += near[i]
            lrs[1, i, pl.ds(SIDE - SUB, SUB), lanes] += far[i]
        for side in range(2):
            for b in range(0, SIDE, SUB):
                head, tail = row_parts(xh, w, half, b + side * (width - SIDE))
                for d in range(DEPTH):
                    lrs[side, d, pl.ds(b, SUB), lanes] += head[d]
                    lrs[side, rows - 1 - d, pl.ds(b, SUB), lanes] += tail[d]
    flat = (2 * rows * SIDE, chans)
    both = lambda a, b: jnp.stack([a[0], b[0]]).reshape(flat)
    section, dconv = cells_of(lrs[...].reshape(flat), both(xl, xr), both(gl, gr), *mats)
    section = section.reshape(2, rows, SIDE, chans)
    dconv = dconv.reshape(2, rows, SIDE, chans)
    sl[0] = section[0]
    sr[0] = section[1]
    dl[0] = dconv[0]
    dr[0] = dconv[1]

    @pl.when(flags[0] + flags[1] > 0)
    def _():
        at = [jnp.where(first, d, SUB - 1 - d) for d in range(DEPTH)]
        whole_at = [jnp.where(first, d, rows - 1 - d) for d in range(DEPTH)]
        mid = pl.ds(SIDE, inner)
        for d in range(DEPTH):
            ends[d] = ce[0, at[d], mid, :]
        widen_rows(xh, 0, strip, DEPTH, SUB)
        for half in range(chans // LANES):
            for p in range(TAPS):
                given = pl.ds(TAPS * jnp.where(first, p, TAPS - 1 - p), TAPS)
                we[half, pl.ds(TAPS * p, TAPS), :] = w[half, given, :]
                wte[half, pl.ds(TAPS * p, TAPS), :] = wt[half, given, :]
        for half in range(chans // LANES):
            lanes = pl.ds(half * LANES, LANES)

            def one(block, carry):
                for k in range(2):
                    start = pl.multiple_of((2 * block + k) * SUB, SUB)
                    parts = end_parts(xh, we, half, start + SIDE)
                    for d in range(DEPTH):
                        ends[d, pl.ds(start, SUB), lanes] += parts[d]
                return carry

            lax.fori_loop(0, inner // (2 * SUB), one, 0)
        rim = lambda ref: jnp.stack([ref[0, at[d], mid, :] for d in range(DEPTH)]).reshape(DEPTH * inner, chans)
        dconv = cells_of(ends[...].reshape(DEPTH * inner, chans), rim(xe), rim(ge), *mats)[1]
        dends[...] = dconv.reshape(DEPTH, inner, chans)
        for half in range(chans // LANES):
            lanes = pl.ds(half * LANES, LANES)
            for d in range(DEPTH):
                xh[half, d, pl.ds(SUB, SIDE), :] = dl[0, whole_at[d], :, lanes].astype(jnp.float32)
                xh[half, d, pl.ds(SUB + SIDE, inner), :] = dends[d, :, lanes].astype(jnp.float32)
                xh[half, d, pl.ds(SUB + SIDE + inner, SIDE), :] = dr[0, whole_at[d], :, lanes].astype(jnp.float32)

            def one_strip(block, carry):
                for k in range(2):
                    start = pl.multiple_of((2 * block + k) * SUB, SUB)
                    out = [None] * DEPTH
                    for q in range(TAPS):
                        for edge in range(DEPTH):
                            x = xh[half, edge, pl.ds(start + SUB - DEPTH + q, SUB), :]
                            for d in range(DEPTH - edge):
                                out[d] = plus(out[d], x * wte[half, pl.ds(TAPS * (edge + d + 4) + q, 1), :])
                    for d in range(DEPTH):
                        xh[half, DEPTH + d, pl.ds(start + SUB, SUB), :] = out[d]
                return carry

            lax.fori_loop(0, width // (2 * SUB), one_strip, 0)
            for d in range(DEPTH):
                tb[0, d, :, lanes] = xh[half, DEPTH + d, pl.ds(SUB, width), :].astype(jnp.bfloat16)


def strip_kernel(left, right, wt, near_ref, far_ref, xcl, xcr):
    rows, chans = near_ref.shape[1], near_ref.shape[3]
    for half in range(chans // LANES):
        lanes = pl.ds(half * LANES, LANES)
        zeros = jnp.zeros((rows + 2 * DEPTH, SUB, LANES), jnp.float32)
        xcl[half, :, pl.ds(0, SUB), :] = zeros
        xcl[half, :, pl.ds(SUB, SUB), :] = left[0, :, :, lanes].astype(jnp.float32)
        xcr[half, :, pl.ds(0, SUB), :] = right[0, :, :, lanes].astype(jnp.float32)
        xcr[half, :, pl.ds(SUB, SUB), :] = zeros
    for half in range(chans // LANES):
        lanes = pl.ds(half * LANES, LANES)
        near = column_parts(xcl, wt, half, [(q, q - DEPTH) for q in range(4, TAPS)])
        far = column_parts(xcr, wt, half, [(q, SUB - DEPTH + q) for q in range(DEPTH)])
        for i in range(rows):
            near_ref[0, i, :, lanes] = near[i]
            far_ref[0, i, :, lanes] = far[i]


def interior_kernel(
    conv, x, cot, top, bot, sl, sr, dl, dr, w, vec, bi, wi, wo, wot, wit, sec, dc, xh, cs, acts, dpres
):
    rows, width, chans = conv.shape[1:]
    inner = width - 2 * SIDE
    mid = pl.ds(SIDE, inner)
    mats = (vec, bi, wi, wo, wot, wit, acts, dpres)
    for full, near, far in ((sec, sl, sr), (dc, dl, dr)):
        full[0, :, pl.ds(0, SIDE), :] = near[0]
        full[0, :, pl.ds(width - SIDE, SIDE), :] = far[0]
    clear_pads(xh, width)
    widen_rows(xh, 0, top, DEPTH, SUB)
    widen_rows(xh, DEPTH, bot, DEPTH, SUB)
    cs[...] = conv[0, :, mid, :]
    for half in range(chans // LANES):
        lanes = pl.ds(half * LANES, LANES)

        def one(block, carry):
            start = pl.multiple_of(block * SUB, SUB)
            head, tail = row_parts(xh, w, half, start + SIDE)
            for d in range(DEPTH):
                cs[d, pl.ds(start, SUB), lanes] += head[d]
                cs[rows - 1 - d, pl.ds(start, SUB), lanes] += tail[d]
            return carry

        lax.fori_loop(0, inner // SUB, one, 0)
    step = SUB

    def some(block, carry):
        flat = (step * inner, chans)
        these = pl.ds(block * step, step)
        section, dconv = cells_of(
            cs[these].reshape(flat), x[0, these, mid, :].reshape(flat), cot[0, these, mid, :].reshape(flat), *mats
        )
        sec[0, these, mid, :] = section.reshape(step, inner, chans)
        dc[0, these, mid, :] = dconv.reshape(step, inner, chans)
        return carry

    lax.fori_loop(0, rows // step, some, 0)


def join_kernel(grad, cot, above, below, top, bot, left, right, wt, out, xh, total):
    rows, width, chans = grad.shape[1:]
    clear_pads(xh, width)
    widen_rows(xh, 0, above, DEPTH, SUB)
    widen_rows(xh, DEPTH, below, DEPTH, SUB)
    total[pl.ds(0, DEPTH)] = grad[0, pl.ds(0, DEPTH)] + top[0].astype(jnp.float32)
    total[pl.ds(DEPTH, DEPTH)] = grad[0, pl.ds(rows - DEPTH, DEPTH)] + bot[0].astype(jnp.float32)
    for half in range(chans // LANES):
        lanes = pl.ds(half * LANES, LANES)

        def one(block, carry):
            start = pl.multiple_of(block * SUB, SUB)
            head, tail = row_parts(xh, wt, half, start)
            for d in range(DEPTH):
                total[d, pl.ds(start, SUB), lanes] += head[d]
                total[2 * DEPTH - 1 - d, pl.ds(start, SUB), lanes] += tail[d]
            return carry

        lax.fori_loop(0, width // SUB, one, 0)

    def finish(row, sums):
        def store(at, values):
            conv_grad = values.astype(jnp.bfloat16).astype(jnp.float32)
            out[0, row, at, :] = (cot[0, row, at, :].astype(jnp.float32) + conv_grad).astype(jnp.bfloat16)

        near, far = pl.ds(0, SIDE), pl.ds(width - SIDE, SIDE)
        mid = pl.ds(SIDE, width - 2 * SIDE)
        store(mid, sums(mid))
        store(near, sums(near) + left[0, row].astype(jnp.float32))
        store(far, sums(far) + right[0, row].astype(jnp.float32))

    def free(row, carry):
        finish(row, lambda at: grad[0, row, at, :])
        return carry

    lax.fori_loop(DEPTH, rows - DEPTH, free, 0)
    for d in range(DEPTH):
        finish(d, lambda at: total[d, at, :])
        finish(rows - DEPTH + d, lambda at: total[DEPTH + d, at, :])


def by_slot(x, base=0):
    return pl.BlockSpec((1,) + tuple(x.shape[1:]), lambda s, *_: (s + base if base else s,) + (0,) * (len(x.shape) - 1))


def whole(x):
    return pl.BlockSpec(tuple(x.shape), lambda s, *_: (0,) * len(x.shape))


def run(kernel, name, span, ins, specs, outs, scratch, flags=None, micros=10, into=(), halves=()):
    base, slots = span
    prefetch = () if flags is None else (flags,)
    first = len(prefetch) + len(ins)

    def body(*refs):
        return kernel(*refs[:first], *refs[first + len(into) :])

    return pl.pallas_call(
        body,
        grid_spec=pltpu.PrefetchScalarGridSpec(
            num_scalar_prefetch=len(prefetch),
            grid=(slots,),
            in_specs=specs + [pl.BlockSpec(memory_space=pl.ANY)] * len(into),
            out_specs=[by_slot(o, base) for o in outs],
            scratch_shapes=[pltpu.VMEM(s, jnp.float32) for s in scratch] + [pltpu.VMEM(s, jnp.bfloat16) for s in halves],
        ),
        out_shape=list(outs),
        input_output_aliases={first + k: k for k in range(len(into))},
        compiler_params=pltpu.CompilerParams(vmem_limit_bytes=60 * 1024 * 1024),
        cost_estimate=pl.CostEstimate(
            flops=micros * 1_000_000_000, transcendentals=0, bytes_accessed=sum(o.size * 2 for o in outs)
        ),
        name=name,
    )(*prefetch, *ins, *into)


def conv_partial(x, weights, name, span, into=()):
    slots, rows, width, chans = x.shape
    out = jax.ShapeDtypeStruct(x.shape, jnp.float32)
    pads = (chans // LANES, 3 * (rows // 2) + 1, width + 2 * SUB, LANES)
    specs = [by_slot(x, span[0]), whole(weights)]
    return run(conv_partial_kernel, name, span, (x, weights), specs, [out], [pads], micros=9 * span[1], into=into)[0]


def face_all(own):
    groups = lax.axis_size("face")
    send = jnp.broadcast_to(own[None], (groups,) + own.shape)
    return lax.all_to_all(send, "face", split_axis=0, concat_axis=0, tiled=True)


def turn_sides(sides, flip):
    tiles = lax.axis_size("tile")
    mirrored = lax.ppermute(sides, "tile", [(t, tiles - 1 - t) for t in range(tiles)])
    return jnp.where(flip[:, :, None, None, None], mirrored[:, :, :, ::-1], sides)


def turn_ends(ends, flip):
    here = jnp.where(lax.axis_index("tile") == 0, flip[:, 0], flip[:, 1])
    return jnp.where(here[:, None, None, None], ends[:, :, ::-1], ends)


def to_neighbours(head, tail):
    tiles, chans = lax.axis_size("tile"), head.shape[-1]
    after = jnp.arange(tiles, dtype=jnp.int32) == lax.axis_index("tile") + 1
    rows = jnp.where(after[:, None, None], tail.reshape(1, -1, chans), head.reshape(1, -1, chans))
    return jnp.pad(rows, ((0, 0), (0, -rows.shape[1] % 8), (0, 0)))


def from_neighbours(got, shape):
    tiles, tile = lax.axis_size("tile"), lax.axis_index("tile")
    count = 1
    for extent in shape[:-1]:
        count *= extent
    above = lax.dynamic_index_in_dim(got, jnp.maximum(tile - 1, 0), 0, False)[:count].reshape(shape)
    below = lax.dynamic_index_in_dim(got, jnp.minimum(tile + 1, tiles - 1), 0, False)[:count].reshape(shape)
    return jnp.where(tile == 0, 0, above), jnp.where(tile == tiles - 1, 0, below)


def spread_ends(ends, rider):
    slots, _, width, chans = ends.shape
    tiles = lax.axis_size("tile")
    rows = width // tiles
    send = jnp.moveaxis(ends.reshape(slots, DEPTH, tiles, rows, chans), 2, 0).reshape(tiles, -1, chans)
    send = jnp.concatenate([send, rider], axis=1)
    got = lax.all_to_all(send, "tile", split_axis=0, concat_axis=0, tiled=True)
    count = slots * DEPTH * rows
    found = jnp.stack([got[0, :count], got[tiles - 1, :count]]).reshape(2, slots, DEPTH, rows, chans)
    return jnp.moveaxis(found, 0, 1), got[:, count:]


def in_three(values):
    parts = []
    for _ in range(3):
        part = lax.reduce_precision(values, 8, 7)
        parts.append(part.astype(jnp.bfloat16))
        values = values - part
    return jnp.stack(parts)


def pick(found, index):
    groups, slots, _, _, rows, chans = found.shape
    strips = found.reshape(groups * slots * 4, DEPTH, rows, chans)
    return jnp.take(strips, index.reshape(-1), axis=0).reshape(slots, 4, DEPTH, rows, chans)


def gather_ends(found, rider=None):
    slots, _, _, rows, chans = found.shape
    tiles = lax.axis_size("tile")
    half = tiles // 2
    send = jnp.stack([found[:, 0]] * half + [found[:, 1]] * (tiles - half)).reshape(tiles, -1, chans)
    count = send.shape[1]
    if rider is not None:
        send = jnp.concatenate([send, rider], axis=1)
    got = lax.all_to_all(send, "tile", split_axis=0, concat_axis=0, tiled=True)
    ends = got[:, :count].reshape(tiles, slots, DEPTH, rows, chans)
    return jnp.moveaxis(ends, 0, 2).reshape(slots, DEPTH, tiles * rows, chans), got[:, count:]


def halo(first, last):
    tiles = lax.axis_size("tile")
    above = lax.ppermute(last, "tile", [(t, t + 1) for t in range(tiles - 1)])
    below = lax.ppermute(first, "tile", [(t + 1, t) for t in range(tiles - 1)])
    return above, below


def row_shards(
    fields,
    cotangent,
    dw_kernel,
    dw_bias,
    norm_gain,
    norm_bias,
    proj_in,
    bias_in,
    proj_out,
    bias_out,
    layer_scale,
    strip_source,
    strip_flip,
):
    slots, rows, width, chans = fields.shape
    tiles = lax.axis_size("tile")
    tile = lax.axis_index("tile")
    first_tile, last_tile = tile == 0, tile == tiles - 1
    flags = jnp.stack([first_tile, last_tile]).astype(jnp.int32)
    own_samples = lax.axis_index("face") * slots + jnp.arange(slots, dtype=jnp.int32)
    source, mirror = reader_tables(own_samples, strip_source, strip_flip)
    entries = jnp.arange(48, dtype=jnp.int32)
    hits = strip_source[None, :] == entries[:, None]
    reader_of = jnp.sum(jnp.where(hits, entries[None, :], 0), axis=1)
    flip_of = jnp.sum(jnp.where(hits, strip_flip[None, :], 0), axis=1)
    own_strips = (own_samples % 12)[:, None] * 4 + jnp.arange(4, dtype=jnp.int32)[None, :]
    target = (own_samples // 12)[:, None] * 48 + reader_of[own_strips]
    target_mirror = flip_of[own_strips] == 1

    own_taps = jnp.concatenate([dw_kernel, dw_bias[:, None]], axis=1).T
    own_chans = own_taps.shape[1]
    taps_count = TAPS * TAPS + 1
    rider_rows = -(-3 * taps_count * own_chans // chans)
    rider_rows += -rider_rows % 8
    rider = in_three(own_taps).reshape(-1)
    rider = jnp.pad(rider, (0, rider_rows * chans - rider.size)).reshape(rider_rows, chans)
    ends = jnp.where(first_tile, fields[:, :DEPTH], fields[:, : rows - DEPTH - 1 : -1])
    ends = turn_ends(ends, target_mirror[:, :2])
    near_ends, riders = spread_ends(ends, jnp.broadcast_to(rider[None], (tiles,) + rider.shape))
    riders = riders.reshape(tiles, -1)[:, : 3 * taps_count * own_chans].astype(jnp.float32)
    riders = riders.reshape(tiles, 3, taps_count, own_chans)
    taps = (riders[:, 0] + riders[:, 1]) + riders[:, 2]
    taps = jnp.moveaxis(taps, 0, 1).reshape(taps_count, chans)
    taps = jnp.pad(taps, ((0, 6), (0, 0)))
    weights = jnp.moveaxis(taps.reshape(-1, chans // LANES, LANES), 1, 0)
    turned = jnp.pad(weights[:, TAPS * TAPS - 1 :: -1], ((0, 0), (0, 7), (0, 0)))
    shared = shared_taps(taps[: taps_count])
    shared_turned = shared_taps(jnp.pad(taps[TAPS * TAPS - 1 :: -1], ((0, 1), (0, 0))))
    vectors = jnp.stack([norm_gain, norm_bias, 2.0 * bias_out, 0.5 * layer_scale, layer_scale, 0.5 * norm_gain])
    mats = (vectors, bias_in[None], proj_in, proj_out, proj_out.T, proj_in.T)

    side_pair = jnp.stack([fields[:, :, :DEPTH], fields[:, :, : width - DEPTH - 1 : -1]], axis=1)
    sides = turn_sides(jnp.swapaxes(side_pair, 2, 3), target_mirror[:, 2:])
    own = jnp.concatenate([near_ends, sides], axis=1)
    found = face_all(own)
    early, own = lax.optimization_barrier((fields, own))
    above, below = halo(early[:, :DEPTH], early[:, rows - DEPTH :])
    partial = conv_partial(early, shared, "conv_partial", (0, 2))
    partial, found, above, below = lax.optimization_barrier((partial, found, above, below))
    picked = pick(found, source)
    late, picked = lax.optimization_barrier((fields, picked))
    sides = picked[:, 2:]
    rider = to_neighbours(sides[:, :, :, :DEPTH], sides[:, :, :, rows - DEPTH :])
    new_ends, riders = gather_ends(picked[:, :2], rider)
    side_above, side_below = from_neighbours(riders, (slots, 2, DEPTH, DEPTH, chans))
    sides = jnp.concatenate([side_above, sides, side_below], axis=3)
    partial = conv_partial(late, shared, "conv_partial_rest", (2, slots - 2), (partial,))
    sides = jnp.swapaxes(sides, 2, 3)
    left = jnp.pad(sides[:, 0, :, ::-1], ((0, 0), (0, 0), (SUB - DEPTH, 0), (0, 0)))
    right = jnp.pad(sides[:, 1], ((0, 0), (0, 0), (0, SUB - DEPTH), (0, 0)))
    top = jnp.where(first_tile, new_ends[:, ::-1], above)
    bot = jnp.where(last_tile, new_ends, below)

    near_spec = pl.BlockSpec((1, rows, SIDE, chans), lambda s, f: (s, 0, 0, 0))
    far_spec = pl.BlockSpec((1, rows, SIDE, chans), lambda s, f: (s, 0, width // SIDE - 1, 0))
    end_spec = pl.BlockSpec((1, SUB, width, chans), lambda s, f: (s, f[1] * (rows // SUB - 1), 0, 0))
    side_out = jax.ShapeDtypeStruct((slots, rows, SIDE, chans), jnp.bfloat16)
    strip_out = jax.ShapeDtypeStruct((slots, DEPTH, width, chans), jnp.bfloat16)
    halves = chans // LANES
    halo_pads = (halves, 2 * DEPTH, width + 2 * SUB, LANES)
    side_pads = (halves, rows + 2 * DEPTH, 2 * SUB, LANES)
    extras = (top, bot, left, right, new_ends[:, ::-1])
    hidden = proj_in.shape[1]
    sl, sr, dl, dr, tb = run(
        edge_kernel,
        "edge_cells",
        (0, slots),
        (partial,) * 3 + (fields,) * 3 + (cotangent,) * 3 + extras + (weights, turned) + mats,
        [near_spec, far_spec, end_spec] * 3 + [by_slot(x) for x in extras] + [whole(x) for x in (weights, turned) + mats],
        [side_out, side_out, side_out, side_out, strip_out],
        [halo_pads, side_pads, side_pads, (2, rows, SIDE, chans), (DEPTH, width - 2 * SIDE, chans)]
        + [weights.shape] * 2,
        flags,
        micros=23,
        halves=[(DEPTH, width - 2 * SIDE, chans)] + [(2 * rows * SIDE, hidden)] * 2,
    )

    outer = jnp.stack([dl[:, :, :SUB], dr[:, :, SIDE - SUB :]], axis=1)
    rims = jnp.stack([outer[:, 0, :, :DEPTH], outer[:, 1, :, SUB - DEPTH :]], axis=1)
    near_ends, riders = spread_ends(tb, to_neighbours(rims[:, :, :DEPTH], rims[:, :, rows - DEPTH :]))
    shown = []
    for rim in from_neighbours(riders, (slots, 2, DEPTH, DEPTH, chans)):
        blank = jnp.zeros((slots, DEPTH, SUB - DEPTH, chans), rim.dtype)
        shown.append(
            jnp.stack([jnp.concatenate([rim[:, 0], blank], axis=2), jnp.concatenate([blank, rim[:, 1]], axis=2)], axis=1)
        )
    outer = jnp.concatenate([shown[0], outer, shown[1]], axis=2)
    strip = jax.ShapeDtypeStruct((slots, rows, SUB, chans), jnp.float32)
    ins = (outer[:, 0], outer[:, 1])
    near, far = run(
        strip_kernel,
        "side_strips",
        (0, slots),
        ins + (turned,),
        [by_slot(x) for x in ins] + [whole(turned)],
        [strip, strip],
        [side_pads, side_pads],
    )
    side_pair = jnp.stack([near[:, :, : SUB - DEPTH - 1 : -1], far[:, :, :DEPTH]], axis=1).astype(jnp.bfloat16)
    own = jnp.concatenate([near_ends, jnp.swapaxes(side_pair, 2, 3)], axis=1)
    found = face_all(own)

    full = jax.ShapeDtypeStruct(fields.shape, jnp.bfloat16)
    done = ()
    for span, sign in (((0, 1), tb), ((1, slots - 1), own)):
        gated = lax.optimization_barrier((fields, sign))[0]
        ins = (partial, gated, cotangent, top, bot, sl, sr, dl, dr)
        done = run(
            interior_kernel,
            "interior_cells",
            span,
            ins + (weights,) + mats,
            [by_slot(x, span[0]) for x in ins] + [whole(x) for x in (weights,) + mats],
            [full, full],
            [halo_pads, (rows, width - 2 * SIDE, chans)],
            micros=8 * span[1],
            into=done,
            halves=[(SUB * (width - 2 * SIDE), hidden)] * 2,
        )
    section_out, dconv = done
    above, below = halo(dconv[:, :DEPTH], dconv[:, rows - DEPTH :])
    grad = conv_partial(dconv, shared_turned, "conv_gradient", (0, 1))
    grad, found = lax.optimization_barrier((grad, found))
    picked = pick(found, target)
    late, picked = lax.optimization_barrier((dconv, picked))
    sides = turn_sides(picked[:, 2:], target_mirror[:, 2:])
    ends = turn_ends(gather_ends(picked[:, :2])[0], target_mirror[:, :2])
    grad = conv_partial(late, shared_turned, "conv_gradient_rest", (1, slots - 1), (grad,))

    top = jnp.where(first_tile, ends, 0)
    bot = jnp.where(last_tile, ends[:, ::-1], 0)
    sides = jnp.swapaxes(sides, 2, 3)
    left = jnp.pad(sides[:, 0], ((0, 0), (0, 0), (0, SIDE - DEPTH), (0, 0)))
    right = jnp.pad(sides[:, 1, :, ::-1], ((0, 0), (0, 0), (SIDE - DEPTH, 0), (0, 0)))
    ins = (grad, cotangent, above, below, top, bot, left, right)
    field_grad = run(
        join_kernel,
        "join",
        (0, slots),
        ins + (turned,),
        [by_slot(x) for x in ins] + [whole(turned)],
        [full],
        [halo_pads, (2 * DEPTH, width, chans)],
    )[0]
    return (section_out, field_grad)


def block_of(fields, *rest):
    rows, width, chans = fields.shape[1:]
    if rows % SUB == 0 and rows <= 16 and chans % LANES == 0 and width % SIDE == 0 and width > 4 * SIDE:
        return row_shards(fields, *rest)
    return shards(fields, *rest)


def solution(mesh):
    placed = (
        P("face", "tile", None, None),
        P("face", "tile", None, None),
        P("tile", None),
        P("tile"),
        P(),
        P(),
        P(),
        P(),
        P(),
        P(),
        P(),
        P(),
        P(),
    )
    return jax.shard_map(
        block_of,
        mesh=mesh,
        in_specs=placed,
        out_specs=(P("face", "tile", None, None), P("face", "tile", None, None)),
        check_vma=False,
    )
```
